128 devices in a mesh: face: 4 (over y), sub: 32 (over x, z, core).
Axes of the slice: x: 4, y: 4, z: 4, core: 2. Of those that a mesh axis runs over, the one named last changes fastest.
Arguments:
- field: bfloat16 [3, 4, 128, 128, 256], P(None, 'face', 'sub'), may hold values from -6 to 6
- dw_kernel: float32 [9, 256], replicated, may hold values from -2 to 2
- dw_bias: float32 [256], replicated, may hold values from -3 to 3
- zonal_kernel: float32 [7, 256], replicated, may hold values from -2 to 2
- zonal_bias: float32 [256], replicated, may hold values from -3 to 3
- norm_gain: float32 [256], replicated, may hold values from 0.1 to 1.9
- w_in: bfloat16 [256, 768], replicated, may hold values from -0.375 to 0.375
- w_out: bfloat16 [768, 256], replicated, may hold values from -0.21875 to 0.21875
- layer_scale: float32 [256], replicated, may hold values from 0.5 to 1.5
Outputs:
- output: bfloat16 [3, 4, 128, 128, 256], P(None, 'face', 'sub')
The draws below stay inside these ranges and needn't reach their ends.
All inputs are finite; a program needn't handle non-finite values.
Results may differ from the reference program's by a relative error of at most 0.001.
The reference program's roundings to bfloat16 on the way (of `padded`, `mixed`, `zonal`, `normed` and `hidden`) count: a program that leaves them out, or rounds other values in their place, can miss the bound.
Values may be sent and summed in bfloat16 or wider, within the bound.
A program may use at most 64 MiB of HBM per device.

```python
import jax
import jax.numpy as jnp
from jax import lax

C = 256
HIDDEN_SIZE = 768
TAPS = 7
DILATION = 4
NSIDE = 128
N_FACE = 4


def block_scale(key, extent, cuts, smallest, high):
    factor_of = 1.0
    for axis_at, blocks in cuts:
        draws = jax.random.uniform(jax.random.fold_in(jax.random.fold_in(key, 6), axis_at), (blocks,), jnp.float32, smallest / len(cuts), high / len(cuts))
        factor_of = factor_of * jnp.repeat(jnp.exp(draws), extent[axis_at] // blocks).reshape((-1,) + (1,) * (len(extent) - 1 - axis_at))
    return factor_of


def gaussian(own_key, dims, width, bound, cuts=(), kind=jnp.bfloat16):
    factor_of = block_scale(own_key, dims, cuts, -0.22, 0.18) if cuts else 1.0
    array = jax.random.normal(own_key, dims, jnp.float32) * width * factor_of
    return jnp.minimum(jnp.maximum(array, -bound), bound).astype(kind)


def setup_inputs(seed: int = 0) -> dict:
    seeds = jax.random.split(jax.random.key(seed), 10)
    field = gaussian(seeds[0], (3, N_FACE, NSIDE, NSIDE, C), 1.0, 6.0, ((1, 4), (2, 32)))
    dw_kernel = gaussian(seeds[1], (9, C), 9 ** -0.5, 2.0, (), jnp.float32)
    dw_bias = gaussian(seeds[2], (C,), 0.5, 3.0, (), jnp.float32)
    zonal_kernel = gaussian(seeds[3], (TAPS, C), TAPS ** -0.5, 2.0, (), jnp.float32)
    zonal_bias = gaussian(seeds[4], (C,), 0.5, 3.0, (), jnp.float32)
    norm_gain = jnp.clip(1.0 + 0.18 * jax.random.normal(seeds[5], (C,), jnp.float32), 0.1, 1.9)
    w_in = gaussian(seeds[6], (C, HIDDEN_SIZE), C ** -0.5, 0.375)
    w_out = gaussian(seeds[7], (HIDDEN_SIZE, C), HIDDEN_SIZE ** -0.5, 0.21875)
    layer_scale = jnp.clip(1.0 + 0.1 * jax.random.normal(seeds[8], (C,), jnp.float32), 0.5, 1.5)
    return dict(field=field, dw_kernel=dw_kernel, dw_bias=dw_bias, zonal_kernel=zonal_kernel, zonal_bias=zonal_bias, norm_gain=norm_gain, w_in=w_in, w_out=w_out, layer_scale=layer_scale)


def cycle_place(facet, column, row_pos, side):
    cycle = (facet + 2) * side - column - row_pos - 1
    along = jnp.where(facet == 0, column + cycle - side, jnp.where((facet == 1) & (cycle < 2 * side), column + cycle - 2 * side, column))
    arc_len = jnp.minimum(jnp.minimum(cycle, side), 4 * side - cycle)
    return (cycle, along, arc_len)

def cycle_cell(cycle, along, side):
    north = (cycle < 2 * side) & (along >= cycle - side)
    middle = jnp.logical_not(north) & (along < 3 * side - cycle)
    facet = jnp.where(north, jnp.int32(0), jnp.where(middle, jnp.int32(1), jnp.int32(2)))
    column = jnp.where(north, along - cycle + side, jnp.where(middle & (cycle < 2 * side), along + 2 * side - cycle, along))
    row_pos = (facet + 2) * side - 1 - cycle - column
    return (facet, column, row_pos)

def pad_face(field, facet, quadrant):
    edge_index = NSIDE - 1
    after = (quadrant + 1) % 4
    before = (quadrant + 3) % 4
    inner = field[facet, quadrant]
    if facet == 0:
        left_col = field[1, quadrant, :, edge_index]
        right_col = field[0, after, edge_index, :]
        top_row = field[1, after, edge_index, :]
        bottom_row = field[0, before, :, edge_index]
    elif facet == 1:
        left_col = field[2, before, :, edge_index]
        right_col = field[0, quadrant, :, 0]
        top_row = field[2, quadrant, edge_index, :]
        bottom_row = field[0, before, 0, :]
    else:
        left_col = field[2, before, 0, :]
        right_col = field[1, after, :, 0]
        top_row = field[2, after, :, 0]
        bottom_row = field[1, quadrant, 0, :]
    corner = jnp.zeros((1, C), field.dtype)
    top_row = jnp.concatenate([corner, top_row, corner], 0)
    bottom_row = jnp.concatenate([corner, bottom_row, corner], 0)
    middle_rows = jnp.concatenate([left_col[:, None], inner, right_col[:, None]], 1)
    return jnp.concatenate([top_row[None], middle_rows, bottom_row[None]], 0)

def reference(field, dw_kernel, dw_bias, zonal_kernel, zonal_bias, norm_gain, w_in, w_out, layer_scale):
    side = NSIDE
    tiles_mixed = []
    for facet in range(3):
        for quadrant in range(4):
            padded = pad_face(field, facet, quadrant).astype(jnp.float32)
            total = jnp.zeros((side, side, C), jnp.float32) + dw_bias
            for i in range(3):
                for j in range(3):
                    total = total + dw_kernel[3 * i + j] * padded[i:i + side, j:j + side]
            tiles_mixed.append(total.astype(jnp.bfloat16))
    mixed = jnp.stack(tiles_mixed).reshape(12 * side * side, C)
    row_pos = lax.broadcasted_iota(jnp.int32, (side, side), 0)
    column = lax.broadcasted_iota(jnp.int32, (side, side), 1)
    half = TAPS // 2
    results = []
    for facet in range(3):
        for quadrant in range(4):
            cycle, along, arc_len = cycle_place(jnp.int32(facet), column, row_pos, side)
            place = quadrant * arc_len + along
            total = jnp.zeros((side * side, C), jnp.float32) + zonal_bias
            for k in range(TAPS):
                moved = (place + DILATION * (k - half)) % (4 * arc_len)
                quad_new = moved // arc_len
                along_new = moved % arc_len
                facet_new, column_new, row_new = cycle_cell(cycle, along_new, side)
                index = ((facet_new * 4 + quad_new) * side + row_new) * side + column_new
                gathered = jnp.take(mixed, index.reshape(-1).astype(jnp.int32), axis=0)
                total = total + zonal_kernel[k] * gathered.astype(jnp.float32)
            zonal = total.astype(jnp.bfloat16)
            values = zonal.astype(jnp.float32)
            mean = lax.optimization_barrier(jnp.mean(values, -1, keepdims=True))
            spread = lax.optimization_barrier(jnp.mean(jnp.square(values - mean), -1, keepdims=True))
            normed = ((values - mean) * lax.rsqrt(spread + 1e-06) * norm_gain).astype(jnp.bfloat16)
            hidden = jax.nn.gelu(jnp.dot(normed, w_in, preferred_element_type=jnp.float32), approximate=False).astype(jnp.bfloat16)
            branch = jnp.dot(hidden, w_out, preferred_element_type=jnp.float32)
            source = field[facet, quadrant].reshape(side * side, C).astype(jnp.float32)
            results.append((source + layer_scale * branch).astype(jnp.bfloat16))
    return jnp.stack(results).reshape(3, 4, side, side, C)
```

```python
import functools

import jax
import jax.numpy as jnp
import numpy as np
from jax import lax
from jax.experimental import pallas as pl
from jax.experimental.pallas import tpu as pltpu
from jax.sharding import PartitionSpec as P

MESH = pl.DeviceIdType.MESH
TAPS = 7
SIDE = 128
ALL = 128
LANES = 128
VP = 385
UP = 257
BASE_N = 288
LIN_ROWS = 1664
ZROWS = 1072


def place_of(index):
    return index // 32, lax.rem(index, 32)


def peer_at(face, sub, step):
    x = sub // 8
    z = lax.rem(sub // 2, 4)
    core = lax.rem(sub, 2)
    pf = lax.rem(face + lax.rem(step, 4), 4)
    px = lax.rem(x + lax.rem(step // 4, 4), 4)
    pz = lax.rem(z + lax.rem(step // 16, 4), 4)
    pc = lax.rem(core + step // 64, 2)
    return pf, px * 8 + pz * 2 + pc


def enter(face, sub):
    barrier = pltpu.get_barrier_semaphore()

    def greet(i, carry):
        pf, ps = peer_at(face, sub, ALL - i)
        pl.semaphore_signal(barrier, inc=1, device_id=(pf, ps), device_id_type=MESH)
        return carry

    lax.fori_loop(1, ALL, greet, 0)
    pl.semaphore_wait(barrier, ALL - 1)


def exchange(face, sub, me, source, target, send_sem, recv_sem):
    def issue(i, carry):
        pf, ps = peer_at(face, sub, ALL - i)
        pltpu.make_async_remote_copy(
            source.at[pf * 32 + ps],
            target.at[me],
            send_sem,
            recv_sem,
            device_id=(pf, ps),
            device_id_type=MESH,
        ).start()
        return carry

    lax.fori_loop(1, ALL, issue, 0)
    target[me] = source[me]


def settle(face, sub, source, target, send_sem, recv_sem):
    whole = pltpu.make_async_remote_copy(
        source.at[pl.ds(0, ALL - 1)],
        target.at[pl.ds(0, ALL - 1)],
        send_sem,
        recv_sem,
        device_id=(face, sub),
        device_id_type=MESH,
    )
    whole.wait_send()
    whole.wait_recv()


def kernel(
    mixed_ref, field_ref, zk_ref, zb_ref, gain_ref, w_in_ref, w_out_ref, ls_ref, out_ref,
    turned, send, recv, chain1, chain2, polar, lin, zlin, back_send, back_recv, unturned,
    send_sem, recv_sem,
):
    face = lax.axis_index("face")
    sub = lax.axis_index("sub")
    me = face * 32 + sub
    enter(face, sub)

    for f in range(3):
        for j in range(4):
            y = sub * 4 + j
            for h in range(2):
                rows = mixed_ref[f, j, :, h * LANES : (h + 1) * LANES].astype(jnp.float32)
                base = (f * 8 + j * 2 + h) * VP
                turned[pl.ds(base + y, SIDE), :] = rows
                turned[pl.ds(base + y + SIDE, SIDE), :] = rows

    def pack(c, carry):
        for f in range(3):
            cells = turned[pl.ds(f * 8 * VP + SIDE + c, 8, stride=VP), :]
            send[c, f] = cells.astype(jnp.bfloat16)
        return carry

    lax.fori_loop(0, ALL, pack, 0, unroll=8)
    exchange(face, sub, me, send, recv, send_sem.at[0], recv_sem.at[0])
    settle(face, sub, send, recv, send_sem.at[0], recv_sem.at[0])

    c = me
    row_in = lax.broadcasted_iota(jnp.int32, (8, LANES), 0) // 2

    def unpack(i, carry):
        q = i // 32
        s = lax.rem(i, 32)
        at = (3 - q) * 32 + s
        upper = row_in + 4 * s > c
        north = recv[i, 0].astype(jnp.float32)
        middle = recv[i, 1].astype(jnp.float32)
        south = recv[i, 2].astype(jnp.float32)
        chain1[at + 3] = jnp.where(upper, middle, north)
        before = recv[lax.rem(i + 96, ALL), 2].astype(jnp.float32)
        chain2[at + 3] = jnp.where(upper, before, middle)
        polar[pl.ds(pl.multiple_of(8 * i, 8), 8), :] = jnp.where(upper, north, south)
        return carry

    lax.fori_loop(0, ALL, unpack, 0, unroll=4)
    for chain in (chain1, chain2):
        for e in range(3):
            chain[e] = chain[ALL + e]
            chain[ALL + 3 + e] = chain[3 + e]

    arc_n = SIDE - 1 - c
    arc_s = c + 1
    base_s = BASE_N + 8 * arc_n + 48
    for q in range(4):
        lin[pl.ds(BASE_N + (3 - q) * 2 * arc_n - 2 * (c + 1), 256), :] = polar[
            q * 256 : (q + 1) * 256, :
        ]
    for q in (3, 2, 1, 0):
        lin[pl.ds(base_s + (3 - q) * 2 * arc_s, 256), :] = polar[q * 256 : (q + 1) * 256, :]
    for base, size in ((BASE_N, 8 * arc_n), (base_s, 8 * arc_s)):
        for e in range(3):
            lin[pl.ds(base + size + 8 * e, 8), :] = lin[pl.ds(base + 8 * e, 8), :]
        for e in range(1, 4):
            lin[pl.ds(base - 8 * e, 8), :] = lin[pl.ds(base - 8 * e + size, 8), :]

    def coeff(ref, k):
        lo = jnp.broadcast_to(ref[k : k + 1, :LANES], (8, LANES))
        hi = jnp.broadcast_to(ref[k : k + 1, LANES:], (8, LANES))
        odd = lax.rem(lax.broadcasted_iota(jnp.int32, (8, LANES), 0), 2) == 1
        return jnp.where(odd, hi, lo)

    taps = [coeff(zk_ref, k) for k in range(TAPS)]
    bias = coeff(zb_ref, 0)

    def stencil_lin(v, carry):
        at = pl.multiple_of(BASE_N + 8 * v, 8)
        total = bias
        for k in range(TAPS):
            total = total + taps[k] * lin[pl.ds(pl.multiple_of(at - 8 * (k - 3), 8), 8), :]
        zlin[pl.ds(at, 8), :] = total
        return carry

    lax.fori_loop(0, ZROWS // 8, stencil_lin, 0, unroll=2)
    row_256 = lax.broadcasted_iota(jnp.int32, (256, LANES), 0) // 2
    for q in range(4):
        from_n = zlin[pl.ds(BASE_N + (3 - q) * 2 * arc_n - 2 * (c + 1), 256), :]
        from_s = zlin[pl.ds(base_s + (3 - q) * 2 * arc_s, 256), :]
        polar[q * 256 : (q + 1) * 256, :] = jnp.where(row_256 > c, from_n, from_s)

    def finish_zonal(i, carry):
        q = i // 32
        s = lax.rem(i, 32)
        at = (3 - q) * 32 + s
        upper = row_in + 4 * s > c
        z1 = bias
        z2 = bias
        for k in range(TAPS):
            z1 = z1 + taps[k] * chain1[at + 6 - k]
            z2 = z2 + taps[k] * chain2[at + 6 - k]
        zp = polar[pl.ds(pl.multiple_of(8 * i, 8), 8), :]
        back_send[i, 0] = jnp.where(upper, zp, z1).astype(jnp.bfloat16)
        back_send[i, 1] = jnp.where(upper, z1, z2).astype(jnp.bfloat16)
        west = lax.rem(i + 96, ALL)
        zp = polar[pl.ds(pl.multiple_of(8 * west, 8), 8), :]
        back_send[west, 2] = jnp.where(upper, z2, zp).astype(jnp.bfloat16)
        return carry

    lax.fori_loop(0, ALL, finish_zonal, 0, unroll=2)
    exchange(face, sub, me, back_send, back_recv, send_sem.at[1], recv_sem.at[1])
    settle(face, sub, back_send, back_recv, send_sem.at[1], recv_sem.at[1])

    def unturn(i, carry):
        for f in range(3):
            cells = back_recv[i, f].astype(jnp.float32)
            unturned[pl.ds(f * 8 * UP + i, 8, stride=UP), :] = cells
            unturned[pl.ds(f * 8 * UP + i + SIDE, 8, stride=UP), :] = cells
        return carry

    lax.fori_loop(0, ALL, unturn, 0, unroll=8)

    gain = gain_ref[...]
    scale = ls_ref[...]
    w_in = w_in_ref[...]
    w_out = w_out_ref[...]

    def mlp(t, carry):
        f = t // 4
        j = lax.rem(t, 4)
        y = sub * 4 + j
        base = (f * 8 + j * 2) * UP + y
        values = jnp.concatenate(
            [unturned[pl.ds(base, SIDE), :], unturned[pl.ds(base + UP, SIDE), :]], axis=1
        )
        mean = jnp.mean(values, -1, keepdims=True)
        centred = values - mean
        spread = jnp.mean(jnp.square(centred), -1, keepdims=True)
        normed = (centred * lax.rsqrt(spread + 1e-06) * gain).astype(jnp.bfloat16)
        pre = jnp.dot(normed, w_in, preferred_element_type=jnp.float32)
        hidden = (0.5 * pre * (1.0 + lax.erf(pre * np.float32(np.sqrt(0.5))))).astype(jnp.bfloat16)
        branch = jnp.dot(hidden, w_out, preferred_element_type=jnp.float32)
        result = field_ref[f, j].astype(jnp.float32) + scale * branch
        out_ref[f, j] = result.astype(jnp.bfloat16)
        return carry

    lax.fori_loop(0, 12, mlp, 0)


def run(mixed, local_field, zonal_kernel, zonal_bias, norm_gain, w_in, w_out, layer_scale):
    vmem = pl.BlockSpec(memory_space=pltpu.VMEM)
    cells = pltpu.VMEM((ALL, 3, 8, LANES), jnp.bfloat16)
    return pl.pallas_call(
        kernel,
        out_shape=jax.ShapeDtypeStruct(local_field.shape, jnp.bfloat16),
        in_specs=[vmem] * 8,
        out_specs=vmem,
        scratch_shapes=[
            pltpu.VMEM((24 * VP, LANES), jnp.float32),
            cells,
            cells,
            pltpu.VMEM((ALL + 6, 8, LANES), jnp.float32),
            pltpu.VMEM((ALL + 6, 8, LANES), jnp.float32),
            pltpu.VMEM((1024, LANES), jnp.float32),
            pltpu.VMEM((LIN_ROWS, LANES), jnp.float32),
            pltpu.VMEM((LIN_ROWS, LANES), jnp.float32),
            cells,
            cells,
            pltpu.VMEM((24 * UP, LANES), jnp.float32),
            pltpu.SemaphoreType.DMA((2,)),
            pltpu.SemaphoreType.DMA((2,)),
        ],
        compiler_params=pltpu.CompilerParams(
            collective_id=0, has_side_effects=True, vmem_limit_bytes=56 * 1024 * 1024
        ),
    )(
        mixed, local_field, zonal_kernel, zonal_bias[None], norm_gain[None], w_in, w_out,
        layer_scale[None],
    )


def extended_2(block, sides, width, periodic):
    for axis, dim in sides:
        count = lax.axis_size(axis)
        forward = [(i, i + 1) for i in range(count - 1)]
        if periodic:
            forward.append((count - 1, 0))
        backward = [(target, source) for source, target in forward]
        low = lax.ppermute(
            lax.slice_in_dim(block, block.shape[dim] - width, None, axis=dim), axis, forward
        )
        high = lax.ppermute(lax.slice_in_dim(block, 0, width, axis=dim), axis, backward)
        block = jnp.concatenate([low, block, high], axis=dim)
    return block


def cut_along(value, dim, size):
    before, after = (value.shape[:dim], value.shape[dim + 1 :])
    return jnp.moveaxis(value.reshape(*before, size, -1, *after), dim, 0)


def sum_at_owner(value, axis, dim):
    parts = cut_along(value, dim, lax.axis_size(axis))
    arrived = lax.all_to_all(parts, axis, split_axis=0, concat_axis=0, tiled=True)
    return arrived.astype(jnp.float32).sum(axis=0)


def joined_along(parts, dim):
    dims = list(parts.shape[1:])
    dims[dim] *= parts.shape[0]
    return jnp.moveaxis(parts, 0, dim).reshape(dims)


def copy_for_each(value, axis):
    size = lax.axis_size(axis)
    return lax.all_to_all(
        jnp.broadcast_to(value[None], (size, *value.shape)), axis, 0, 0, tiled=True
    )


def gathered_copies(value, axis, dim):
    return joined_along(copy_for_each(value, axis), dim)


def shards(
    field, dw_kernel, dw_bias, zonal_kernel, zonal_bias, norm_gain, w_in, w_out, layer_scale
):
    local_field = field[:, 0]
    rows_here = local_field.shape[1]
    side_cells = local_field.shape[2]
    channels = local_field.shape[3]
    edge_index = side_cells - 1
    sub_count = lax.axis_size("sub")
    quad_total = lax.axis_size("face")
    sub_index = lax.axis_index("sub")
    quad_index = lax.axis_index("face")
    row_start = sub_index * rows_here
    side_pair = jnp.stack([local_field[1, :, 0], local_field[2, :, edge_index]])
    beside_all = extended_2(side_pair, (("face", 0),), 1, True)
    last_lines = jnp.where(
        sub_index == sub_count - 1, local_field[:, rows_here - 1], jnp.zeros_like(local_field[:, 0])
    )
    first_lines = jnp.where(sub_index == 0, local_field[:, 0], jnp.zeros_like(local_field[:, 0]))
    rim_lines = jnp.swapaxes(jnp.concatenate([last_lines, first_lines], 0), 0, 1)
    pieces = sum_at_owner(rim_lines.astype(jnp.float32).astype(jnp.bfloat16), "sub", 0).astype(
        jnp.bfloat16
    )
    strips = jnp.stack(
        [
            pieces[:, 0],
            pieces[:, 1],
            local_field[2, :, 0],
            pieces[:, 5],
            local_field[0, :, edge_index],
            pieces[:, 3],
        ]
    )
    near = extended_2(strips, (("face", 0),), 3, True)
    wanted = jnp.stack([near[10], pieces[:, 2], near[11], near[1], near[2], pieces[:, 4]])
    lines = gathered_copies(wanted, "sub", 1)
    left_slice = near[0]
    right_slice = near[9]
    face_top = lines[0:3]
    face_bottom = lines[3:6]
    left_side = jnp.stack([local_field[1, :, edge_index], beside_all[0], left_slice])
    right_side = jnp.stack([right_slice, local_field[0, :, 0], beside_all[3]])
    widened = jnp.concatenate([left_side[:, :, None], local_field, right_side[:, :, None]], 2)
    extended = extended_2(widened, (("sub", 1),), 1, False)
    corner = jnp.zeros((3, 1, channels), local_field.dtype)
    face_top = jnp.concatenate([corner, face_top, corner], 1)
    face_bottom = jnp.concatenate([corner, face_bottom, corner], 1)
    first_row = jnp.where(sub_index == 0, face_top, extended[:, 0])
    final_row = jnp.where(sub_index == sub_count - 1, face_bottom, extended[:, rows_here + 1])
    padded = jnp.concatenate(
        [first_row[:, None], extended[:, 1 : rows_here + 1], final_row[:, None]], 1
    )
    total = jnp.zeros((3, rows_here, side_cells, channels), jnp.float32) + dw_bias
    for i in range(3):
        for j in range(3):
            total = total + dw_kernel[3 * i + j] * padded[
                :, i : i + rows_here, j : j + side_cells
            ].astype(jnp.float32)
    mixed = total.astype(jnp.bfloat16)
    output = run(
        mixed, local_field, zonal_kernel, zonal_bias, norm_gain, w_in, w_out, layer_scale
    )
    return output[:, None]


def solution(mesh):
    in_specs = (P(None, "face", "sub", None, None), P(), P(), P(), P(), P(), P(), P(), P())
    out_specs = P(None, "face", "sub", None, None)
    return jax.shard_map(shards, mesh=mesh, in_specs=in_specs, out_specs=out_specs, check_vma=False)
```

```python
import functools

import jax
import jax.numpy as jnp
import numpy as np
from jax import lax
from jax.experimental import pallas as pl
from jax.experimental.pallas import tpu as pltpu
from jax.sharding import PartitionSpec as P

MESH = pl.DeviceIdType.MESH
TAPS = 7
SIDE = 128
ALL = 128
LANES = 128
PITCH = 137
ROW = 8
TURN = 137
FACE_ROWS = 8 * TURN + 16
BASE_N = 288
LIN_ROWS = 1664
ZROWS = 1072


def place_of(index):
    return index // 32, lax.rem(index, 32)


def peer_at(face, sub, step):
    x = sub // 8
    z = lax.rem(sub // 2, 4)
    core = lax.rem(sub, 2)
    pf = lax.rem(face + lax.rem(step, 4), 4)
    px = lax.rem(x + lax.rem(step // 4, 4), 4)
    pz = lax.rem(z + lax.rem(step // 16, 4), 4)
    pc = lax.rem(core + step // 64, 2)
    return pf, px * 8 + pz * 2 + pc


def announce(face, sub):
    barrier = pltpu.get_barrier_semaphore()

    def greet(i, carry):
        pf, ps = peer_at(face, sub, ALL - i)
        pl.semaphore_signal(barrier, inc=1, device_id=(pf, ps), device_id_type=MESH)
        return carry

    lax.fori_loop(1, ALL, greet, 0)


def exchange(face, sub, me, source, target, send_sem, recv_sem):
    def issue(i, carry):
        pf, ps = peer_at(face, sub, ALL - i)
        pltpu.make_async_remote_copy(
            source.at[pf * 32 + ps],
            target.at[me],
            send_sem,
            recv_sem,
            device_id=(pf, ps),
            device_id_type=MESH,
        ).start()
        return carry

    lax.fori_loop(1, ALL, issue, 0)
    target[me] = source[me]


def settle(face, sub, source, target, send_sem, recv_sem):
    whole = pltpu.make_async_remote_copy(
        source.at[pl.ds(0, ALL - 1)],
        target.at[pl.ds(0, ALL - 1)],
        send_sem,
        recv_sem,
        device_id=(face, sub),
        device_id_type=MESH,
    )
    whole.wait_send()
    whole.wait_recv()


def kernel(
    field_ref, dwk_ref, dwb_ref, zk_ref, zb_ref, gain_ref, w_in_ref, w_out_ref, ls_ref, out_ref,
    grid, row_lo, row_hi, cols, left1, right2, pieces, right0, left2, rim_hi, rim_lo, rim_rows,
    turned, send, recv, chain1, chain2, polar, lin, zlin, back_send, back_recv,
    send_sem, recv_sem, row_sent, lo_sem, hi_sem, col_sent, left_sem, right_sem, piece_sent,
    piece_sem, rim_sent, rim_sem,
):
    face = lax.axis_index("face")
    sub = lax.axis_index("sub")
    me = face * 32 + sub
    east = lax.rem(face + 1, 4)
    west = lax.rem(face + 3, 4)
    first = sub == 0
    last = sub == 31
    announce(face, sub)

    def start(f, r, h=0):
        return (f * 12 + r * 2 + h) * PITCH + ROW

    def widen(t, carry):
        f = t // 4
        j = lax.rem(t, 4)
        for h in range(2):
            grid[pl.ds(start(f, j + 1, h), SIDE), :] = field_ref[
                f, j, :, h * LANES : (h + 1) * LANES
            ].astype(jnp.float32)
        return carry

    lax.fori_loop(0, 12, widen, 0)
    for n, (f, x) in enumerate(((2, SIDE - 1), (1, 0), (0, SIDE - 1), (2, 0))):
        cols[n] = grid[pl.ds(start(f, 1) + x, 8, stride=PITCH), :].astype(jnp.bfloat16)

    def cut(base):
        def one(t, carry):
            for h in range(2):
                at = base + h * PITCH + 4 * t - 1
                pieces[t, h] = grid[pl.ds(at, 8), :].astype(jnp.bfloat16)
            return carry

        lax.fori_loop(0, 32, one, 0)

    pl.when(last)(lambda: cut(start(0, 4)))
    pl.when(first)(lambda: cut(start(2, 1)))

    def push(source, target, sent, got, pf, ps):
        return pltpu.make_async_remote_copy(
            source, target, sent, got, device_id=(pf, ps), device_id_type=MESH
        )

    inner = []
    for f in range(3):
        inner.append((sub < 31, push(
            field_ref.at[f, 3], row_lo.at[f], row_sent.at[0, f], lo_sem.at[f], face, sub + 1)))
        inner.append((sub > 0, push(
            field_ref.at[f, 0], row_hi.at[f], row_sent.at[1, f], hi_sem.at[f], face, sub - 1)))
    inner.append((last, push(
        field_ref.at[1, 3], row_lo.at[0], row_sent.at[0, 1], lo_sem.at[0], west, 0)))
    inner.append((last, push(
        field_ref.at[2, 3], row_lo.at[1], row_sent.at[0, 2], lo_sem.at[1], face, 0)))
    inner.append((first, push(
        field_ref.at[0, 0], row_hi.at[1], row_sent.at[1, 0], hi_sem.at[1], east, 31)))
    inner.append((first, push(
        field_ref.at[1, 0], row_hi.at[2], row_sent.at[1, 1], hi_sem.at[2], face, 31)))
    for d, cond in ((-1, sub > 0), (0, sub >= 0), (1, sub < 31)):
        inner.append((cond, push(
            cols.at[0], left1.at[1 - d], col_sent.at[0, 1 - d], left_sem.at[1 - d], east, sub + d)))
        inner.append((cond, push(
            cols.at[1], right2.at[1 - d], col_sent.at[1, 1 - d], right_sem.at[1 - d], west, sub + d)))
    inner.append((sub >= 0, push(
        cols.at[2], rim_hi.at[sub], rim_sent.at[0], rim_sem.at[0], east, 31)))
    inner.append((sub >= 0, push(
        cols.at[3], rim_lo.at[sub], rim_sent.at[1], rim_sem.at[1], west, 0)))

    pl.semaphore_wait(pltpu.get_barrier_semaphore(), ALL - 1)
    for cond, copy in inner:
        pl.when(cond)(copy.start)

    def scatter(pf, target, got):
        def one(t, carry):
            push(pieces.at[t], target, piece_sent, got, pf, t).start()
            return carry

        lax.fori_loop(0, 32, one, 0)

    pl.when(last)(lambda: scatter(west, right0, piece_sem.at[0]))
    pl.when(first)(lambda: scatter(east, left2, piece_sem.at[1]))

    def weight(ref, tap, h):
        return ref[tap : tap + 1, h * LANES : (h + 1) * LANES]

    def partial_sum(total, f, j, h, x, size, rows):
        for i in rows:
            for k in range(3):
                at = start(f, j + i, h) + x + k - 1
                total = total + weight(dwk_ref, 3 * i + k, h) * grid[pl.ds(at, size), :]
        return total

    def slot(f, j, h):
        return f * FACE_ROWS + (2 * j + h) * TURN + j + 8

    def inside(f, carry):
        for j in range(4):
            rows = (1, 2) if j == 0 else (0, 1) if j == 3 else (0, 1, 2)
            for h in range(2):
                for x in (8, 64):
                    zero = jnp.broadcast_to(weight(dwb_ref, 0, h), (56, LANES))
                    turned[pl.ds(slot(f, j, h) + x, 56), :] = partial_sum(
                        zero, f, j, h, x, 56, rows)
        return carry

    lax.fori_loop(0, 3, inside, 0)

    def took(ref, sem):
        push(ref, ref, row_sent.at[0, 0], sem, face, sub).wait_recv()

    for f in range(3):
        pl.when((sub > 0) if f == 2 else (sub >= 0))(
            lambda f=f: took(row_lo.at[f], lo_sem.at[f]))
        pl.when((sub < 31) if f == 0 else (sub >= 0))(
            lambda f=f: took(row_hi.at[f], hi_sem.at[f]))
    took(right0, piece_sem.at[0])
    took(left2, piece_sem.at[1])
    for e, cond in ((0, sub > 0), (1, sub >= 0), (2, sub < 31)):
        pl.when(cond)(lambda e=e: took(left1.at[e], left_sem.at[e]))
        pl.when(cond)(lambda e=e: took(right2.at[e], right_sem.at[e]))

    for f in range(3):
        for h in range(2):
            half = slice(h * LANES, (h + 1) * LANES)
            grid[pl.ds(start(f, 0, h), SIDE), :] = row_lo[f, :, half].astype(jnp.float32)
            grid[pl.ds(start(f, 5, h), SIDE), :] = row_hi[f, :, half].astype(jnp.float32)

    def rim(ref, sem, f, r):
        took(ref, sem)
        rim_rows[...] = ref[...].astype(jnp.float32).reshape(2 * SIDE, LANES)
        for h in range(2):
            grid[pl.ds(start(f, r, h), SIDE), :] = rim_rows[pl.ds(h, SIDE, stride=2), :]

    pl.when(first)(lambda: rim(rim_lo, rim_sem.at[1], 2, 0))
    pl.when(last)(lambda: rim(rim_hi, rim_sem.at[0], 0, 5))

    for r, size in ((0, 8), (4, 4)):
        grid[pl.ds(start(0, r) - 1, size, stride=PITCH), :] = grid[
            pl.ds(start(1, r) + SIDE - 1, size, stride=PITCH), :]
        grid[pl.ds(start(1, r) + SIDE, size, stride=PITCH), :] = grid[
            pl.ds(start(0, r), size, stride=PITCH), :]
    for f, x, ref in ((1, -1, left1), (2, SIDE, right2)):
        before = ref[0].astype(jnp.float32)
        after = ref[2].astype(jnp.float32)
        grid[pl.ds(start(f, 0) + x, 2, stride=PITCH), :] = before[6:8]
        grid[pl.ds(start(f, 1) + x, 8, stride=PITCH), :] = ref[1].astype(jnp.float32)
        grid[pl.ds(start(f, 5) + x, 2, stride=PITCH), :] = after[0:2]
    for f, x, ref in ((0, SIDE, right0), (2, -1, left2)):
        for h in range(2):
            grid[pl.ds(start(f, 0, h) + x, 6, stride=2 * PITCH), :] = ref[h].astype(jnp.float32)[:6]

    def corners(r):
        for f in range(3):
            for x in (-1, SIDE):
                grid[pl.ds(start(f, r) + x, 2, stride=PITCH), :] = jnp.zeros((2, LANES), jnp.float32)

    pl.when(first)(lambda: corners(0))
    pl.when(last)(lambda: corners(5))

    def around(f, carry):
        for j in range(4):
            for h in range(2):
                for x in (0, SIDE - 8):
                    zero = jnp.broadcast_to(weight(dwb_ref, 0, h), (8, LANES))
                    turned[pl.ds(slot(f, j, h) + x, 8), :] = partial_sum(
                        zero, f, j, h, x, 8, (0, 1, 2))
                if j in (0, 3):
                    for x in (8, 64):
                        at = pl.ds(slot(f, j, h) + x, 56)
                        turned[at, :] = partial_sum(
                            turned[at, :], f, j, h, x, 56, (0,) if j == 0 else (2,))
                if j:
                    turned[pl.ds(slot(f, j, h) - j, j), :] = turned[
                        pl.ds(slot(f, j, h) + SIDE - j, j), :]
        return carry

    lax.fori_loop(0, 3, around, 0)

    def pack(t, carry):
        c = lax.rem(t + 4 * sub, ALL)
        for f in range(3):
            cells = turned[pl.ds(f * FACE_ROWS + 8 + t, 8, stride=TURN), :]
            send[c, f] = cells.astype(jnp.bfloat16)
        return carry

    lax.fori_loop(0, ALL, pack, 0, unroll=8)
    exchange(face, sub, me, send, recv, send_sem.at[0], recv_sem.at[0])
    settle(face, sub, send, recv, send_sem.at[0], recv_sem.at[0])
    for cond, copy in inner:
        pl.when(cond)(copy.wait_send)
    pl.when(first | last)(
        lambda: push(pieces, pieces, piece_sent, piece_sem.at[0], face, sub).wait_send())

    c = me
    row_in = lax.broadcasted_iota(jnp.int32, (8, LANES), 0) // 2

    def unpack(i, carry):
        q = i // 32
        s = lax.rem(i, 32)
        at = (3 - q) * 32 + s
        upper = row_in + 4 * s > c
        north = recv[i, 0].astype(jnp.float32)
        middle = recv[i, 1].astype(jnp.float32)
        south = recv[i, 2].astype(jnp.float32)
        chain1[at + 3] = jnp.where(upper, middle, north)
        before = recv[lax.rem(i + 96, ALL), 2].astype(jnp.float32)
        chain2[at + 3] = jnp.where(upper, before, middle)
        polar[pl.ds(pl.multiple_of(8 * i, 8), 8), :] = jnp.where(upper, north, south)
        return carry

    lax.fori_loop(0, ALL, unpack, 0, unroll=4)
    for chain in (chain1, chain2):
        for e in range(3):
            chain[e] = chain[ALL + e]
            chain[ALL + 3 + e] = chain[3 + e]

    arc_n = SIDE - 1 - c
    arc_s = c + 1
    base_s = BASE_N + 8 * arc_n + 48
    for q in range(4):
        lin[pl.ds(BASE_N + (3 - q) * 2 * arc_n - 2 * (c + 1), 256), :] = polar[
            q * 256 : (q + 1) * 256, :
        ]
    for q in (3, 2, 1, 0):
        lin[pl.ds(base_s + (3 - q) * 2 * arc_s, 256), :] = polar[q * 256 : (q + 1) * 256, :]
    for base, size in ((BASE_N, 8 * arc_n), (base_s, 8 * arc_s)):
        for e in range(3):
            lin[pl.ds(base + size + 8 * e, 8), :] = lin[pl.ds(base + 8 * e, 8), :]
        for e in range(1, 4):
            lin[pl.ds(base - 8 * e, 8), :] = lin[pl.ds(base - 8 * e + size, 8), :]

    def coeff(ref, k):
        lo = jnp.broadcast_to(ref[k : k + 1, :LANES], (8, LANES))
        hi = jnp.broadcast_to(ref[k : k + 1, LANES:], (8, LANES))
        odd = lax.rem(lax.broadcasted_iota(jnp.int32, (8, LANES), 0), 2) == 1
        return jnp.where(odd, hi, lo)

    taps = [coeff(zk_ref, k) for k in range(TAPS)]
    bias = coeff(zb_ref, 0)

    def stencil_lin(v, carry):
        at = pl.multiple_of(BASE_N + 8 * v, 8)
        total = bias
        for k in range(TAPS):
            total = total + taps[k] * lin[pl.ds(pl.multiple_of(at - 8 * (k - 3), 8), 8), :]
        zlin[pl.ds(at, 8), :] = total
        return carry

    lax.fori_loop(0, ZROWS // 8, stencil_lin, 0, unroll=2)
    row_256 = lax.broadcasted_iota(jnp.int32, (256, LANES), 0) // 2
    for q in range(4):
        from_n = zlin[pl.ds(BASE_N + (3 - q) * 2 * arc_n - 2 * (c + 1), 256), :]
        from_s = zlin[pl.ds(base_s + (3 - q) * 2 * arc_s, 256), :]
        polar[q * 256 : (q + 1) * 256, :] = jnp.where(row_256 > c, from_n, from_s)

    def finish_zonal(i, carry):
        q = i // 32
        s = lax.rem(i, 32)
        at = (3 - q) * 32 + s
        upper = row_in + 4 * s > c
        z1 = bias
        z2 = bias
        for k in range(TAPS):
            z1 = z1 + taps[k] * chain1[at + 6 - k]
            z2 = z2 + taps[k] * chain2[at + 6 - k]
        zp = polar[pl.ds(pl.multiple_of(8 * i, 8), 8), :]
        back_send[i, 0] = jnp.where(upper, zp, z1).astype(jnp.bfloat16)
        back_send[i, 1] = jnp.where(upper, z1, z2).astype(jnp.bfloat16)
        back = lax.rem(i + 96, ALL)
        zp = polar[pl.ds(pl.multiple_of(8 * back, 8), 8), :]
        back_send[back, 2] = jnp.where(upper, z2, zp).astype(jnp.bfloat16)
        return carry

    lax.fori_loop(0, ALL, finish_zonal, 0, unroll=2)
    exchange(face, sub, me, back_send, back_recv, send_sem.at[1], recv_sem.at[1])
    settle(face, sub, back_send, back_recv, send_sem.at[1], recv_sem.at[1])

    def unturn(i, carry):
        t = lax.rem(i + ALL - 4 * sub, ALL)
        for f in range(3):
            turned[pl.ds(f * FACE_ROWS + 8 + t, 8, stride=TURN), :] = back_recv[i, f].astype(
                jnp.float32)
        return carry

    lax.fori_loop(0, ALL, unturn, 0, unroll=8)
    for f in range(3):
        for j in range(1, 4):
            for h in range(2):
                turned[pl.ds(slot(f, j, h) + SIDE - j, j), :] = turned[
                    pl.ds(slot(f, j, h) - j, j), :]

    gain = gain_ref[...]
    scale = ls_ref[...]
    w_in = w_in_ref[...]
    w_out = w_out_ref[...]

    def mlp(t, carry):
        f = t // 4
        j = lax.rem(t, 4)
        base = f * FACE_ROWS + 2 * j * TURN + j + 8
        values = jnp.concatenate(
            [turned[pl.ds(base, SIDE), :], turned[pl.ds(base + TURN, SIDE), :]], axis=1
        )
        mean = jnp.mean(values, -1, keepdims=True)
        centred = values - mean
        spread = jnp.mean(jnp.square(centred), -1, keepdims=True)
        normed = (centred * lax.rsqrt(spread + 1e-06) * gain).astype(jnp.bfloat16)
        pre = jnp.dot(normed, w_in, preferred_element_type=jnp.float32)
        hidden = (0.5 * pre * (1.0 + lax.erf(pre * np.float32(np.sqrt(0.5))))).astype(jnp.bfloat16)
        branch = jnp.dot(hidden, w_out, preferred_element_type=jnp.float32)
        result = field_ref[f, j].astype(jnp.float32) + scale * branch
        out_ref[f, j] = result.astype(jnp.bfloat16)
        return carry

    lax.fori_loop(0, 12, mlp, 0)


def run(field, dw_kernel, dw_bias, zonal_kernel, zonal_bias, norm_gain, w_in, w_out, layer_scale):
    vmem = pl.BlockSpec(memory_space=pltpu.VMEM)
    cells = pltpu.VMEM((ALL, 3, 8, LANES), jnp.bfloat16)
    lines = pltpu.VMEM((3, SIDE, 2 * LANES), jnp.bfloat16)
    tiles = lambda *lead: pltpu.VMEM((*lead, 8, LANES), jnp.bfloat16)
    rows = lambda n: pltpu.VMEM((n, LANES), jnp.float32)
    dma = pltpu.SemaphoreType.DMA
    return pl.pallas_call(
        kernel,
        out_shape=jax.ShapeDtypeStruct(field.shape, jnp.bfloat16),
        in_specs=[vmem] * 9,
        out_specs=vmem,
        scratch_shapes=[
            rows(36 * PITCH + 16),
            lines,
            lines,
            tiles(4),
            tiles(3),
            tiles(3),
            tiles(32, 2),
            tiles(2),
            tiles(2),
            tiles(32),
            tiles(32),
            rows(2 * SIDE),
            rows(3 * FACE_ROWS + 8),
            cells,
            cells,
            pltpu.VMEM((ALL + 6, 8, LANES), jnp.float32),
            pltpu.VMEM((ALL + 6, 8, LANES), jnp.float32),
            rows(1024),
            rows(LIN_ROWS),
            rows(LIN_ROWS),
            cells,
            cells,
            dma((2,)),
            dma((2,)),
            dma((2, 3)),
            dma((3,)),
            dma((3,)),
            dma((2, 3)),
            dma((3,)),
            dma((3,)),
            dma,
            dma((2,)),
            dma((2,)),
            dma((2,)),
        ],
        compiler_params=pltpu.CompilerParams(
            collective_id=0, has_side_effects=True, vmem_limit_bytes=56 * 1024 * 1024
        ),
    )(
        field, dw_kernel, dw_bias[None], zonal_kernel, zonal_bias[None], norm_gain[None], w_in,
        w_out, layer_scale[None],
    )


def shards(
    field, dw_kernel, dw_bias, zonal_kernel, zonal_bias, norm_gain, w_in, w_out, layer_scale
):
    output = run(
        field[:, 0], dw_kernel, dw_bias, zonal_kernel, zonal_bias, norm_gain, w_in, w_out,
        layer_scale,
    )
    return output[:, None]


def solution(mesh):
    in_specs = (P(None, "face", "sub", None, None), P(), P(), P(), P(), P(), P(), P(), P())
    out_specs = P(None, "face", "sub", None, None)
    return jax.shard_map(shards, mesh=mesh, in_specs=in_specs, out_specs=out_specs, check_vma=False)
```

```python
import functools

import jax
import jax.numpy as jnp
import numpy as np
from jax import lax
from jax.experimental import pallas as pl
from jax.experimental.pallas import tpu as pltpu
from jax.sharding import PartitionSpec as P

MESH = pl.DeviceIdType.MESH
TAPS = 7
SIDE = 128
ALL = 128
LANES = 128
PITCH = 137
ROW = 8
TURN = 137
FACE_ROWS = 8 * TURN + 16
BASE_N = 288
LIN_ROWS = 1664
ZROWS = 1072


def peer_at(face, sub, step):
    pf = (face + step) & 3
    px = ((sub >> 3) + (step >> 2)) & 3
    pz = ((sub >> 1) + (step >> 4)) & 3
    pc = (sub + (step >> 6)) & 1
    return pf, (px << 3) + (pz << 1) + pc


def announce(face, sub):
    barrier = pltpu.get_barrier_semaphore()

    def greet(i, carry):
        pf, ps = peer_at(face, sub, ALL - i)
        pl.semaphore_signal(barrier, inc=1, device_id=(pf, ps), device_id_type=MESH)
        return carry

    lax.fori_loop(1, ALL, greet, 0, unroll=2)


def exchange(face, sub, prepare, source, target, send_sem, recv_sem):
    me = face * 32 + sub

    def push(pf, ps):
        pltpu.make_async_remote_copy(
            source.at[pf * 32 + ps],
            target.at[me],
            send_sem,
            recv_sem,
            device_id=(pf, ps),
            device_id_type=MESH,
        ).start()

    def step(i, carry):
        pf, ps = peer_at(face, sub, ALL - i)
        prepare(pf, ps)
        push(*carry)
        return pf, ps

    pf, ps = peer_at(face, sub, ALL - 1)
    prepare(pf, ps)
    push(*lax.fori_loop(2, ALL, step, (pf, ps), unroll=2))


def settle(face, sub, source, target, send_sem, recv_sem):
    whole = pltpu.make_async_remote_copy(
        source.at[pl.ds(0, ALL - 1)],
        target.at[pl.ds(0, ALL - 1)],
        send_sem,
        recv_sem,
        device_id=(face, sub),
        device_id_type=MESH,
    )
    whole.wait_send()
    whole.wait_recv()


def kernel(
    field_hbm, dwk_hbm, dwb_hbm, zk_hbm, zb_hbm, gain_hbm, w_in_hbm, w_out_hbm, ls_hbm, out_ref,
    field_ref, dwk_ref, dwb_ref, zk_ref, zb_ref, gain_ref, w_in_ref, w_out_ref, ls_ref, load_sem,
    grid, row_lo, row_hi, cols, left1, right2, pieces, right0, left2, rim_hi, rim_lo, rim_rows,
    turned, send, recv, chain1, chain2, polar, lin, zlin, back_send, back_recv,
    send_sem, recv_sem, row_sent, lo_sem, hi_sem, col_sent, left_sem, right_sem, piece_sent,
    piece_sem, rim_sent, rim_sem,
):
    face = lax.axis_index("face")
    sub = lax.axis_index("sub")
    me = face * 32 + sub
    east = (face + 1) & 3
    west = (face + 3) & 3
    first = sub == 0
    last = sub == 31
    loads = [
        pltpu.make_async_copy(source, target, load_sem.at[n])
        for n, (source, target) in enumerate((
            (field_hbm, field_ref), (dwk_hbm, dwk_ref), (dwb_hbm, dwb_ref), (zk_hbm, zk_ref),
            (zb_hbm, zb_ref), (gain_hbm, gain_ref), (w_in_hbm, w_in_ref), (w_out_hbm, w_out_ref),
            (ls_hbm, ls_ref)))
    ]
    loads[0].start()
    announce(face, sub)
    for load in loads[1:]:
        load.start()
    loads[0].wait()

    def start(f, r, h=0):
        return (f * 12 + r * 2 + h) * PITCH + ROW

    def widen(t, carry):
        f = t >> 2
        j = t & 3
        for h in range(2):
            grid[pl.ds(start(f, j + 1, h), SIDE), :] = field_ref[
                f, j, :, h * LANES : (h + 1) * LANES
            ].astype(jnp.float32)
        return carry

    lax.fori_loop(0, 12, widen, 0)
    for n, (f, x) in enumerate(((2, SIDE - 1), (1, 0), (0, SIDE - 1), (2, 0))):
        cols[n] = grid[pl.ds(start(f, 1) + x, 8, stride=PITCH), :].astype(jnp.bfloat16)

    def cut(base):
        def one(t, carry):
            for h in range(2):
                at = base + h * PITCH + 4 * t - 1
                pieces[t, h] = grid[pl.ds(at, 8), :].astype(jnp.bfloat16)
            return carry

        lax.fori_loop(0, 32, one, 0)

    pl.when(last)(lambda: cut(start(0, 4)))
    pl.when(first)(lambda: cut(start(2, 1)))

    def push(source, target, sent, got, pf, ps):
        return pltpu.make_async_remote_copy(
            source, target, sent, got, device_id=(pf, ps), device_id_type=MESH
        )

    inner = []
    for f in range(3):
        inner.append((sub < 31, push(
            field_ref.at[f, 3], row_lo.at[f], row_sent.at[0, f], lo_sem.at[f], face, sub + 1)))
        inner.append((sub > 0, push(
            field_ref.at[f, 0], row_hi.at[f], row_sent.at[1, f], hi_sem.at[f], face, sub - 1)))
    inner.append((last, push(
        field_ref.at[1, 3], row_lo.at[0], row_sent.at[0, 1], lo_sem.at[0], west, 0)))
    inner.append((last, push(
        field_ref.at[2, 3], row_lo.at[1], row_sent.at[0, 2], lo_sem.at[1], face, 0)))
    inner.append((first, push(
        field_ref.at[0, 0], row_hi.at[1], row_sent.at[1, 0], hi_sem.at[1], east, 31)))
    inner.append((first, push(
        field_ref.at[1, 0], row_hi.at[2], row_sent.at[1, 1], hi_sem.at[2], face, 31)))
    for d, cond in ((-1, sub > 0), (0, sub >= 0), (1, sub < 31)):
        inner.append((cond, push(
            cols.at[0], left1.at[1 - d], col_sent.at[0, 1 - d], left_sem.at[1 - d], east, sub + d)))
        inner.append((cond, push(
            cols.at[1], right2.at[1 - d], col_sent.at[1, 1 - d], right_sem.at[1 - d], west, sub + d)))
    inner.append((sub >= 0, push(
        cols.at[2], rim_hi.at[sub], rim_sent.at[0], rim_sem.at[0], east, 31)))
    inner.append((sub >= 0, push(
        cols.at[3], rim_lo.at[sub], rim_sent.at[1], rim_sem.at[1], west, 0)))

    pl.semaphore_wait(pltpu.get_barrier_semaphore(), ALL - 1)
    for cond, copy in inner:
        pl.when(cond)(copy.start)

    def scatter(pf, target, got):
        def one(t, carry):
            push(pieces.at[t], target, piece_sent, got, pf, t).start()
            return carry

        lax.fori_loop(0, 32, one, 0)

    pl.when(last)(lambda: scatter(west, right0, piece_sem.at[0]))
    pl.when(first)(lambda: scatter(east, left2, piece_sem.at[1]))

    for load in loads[1:]:
        load.wait()

    def weight(ref, tap, h):
        return ref[tap : tap + 1, h * LANES : (h + 1) * LANES]

    def partial_sum(total, f, j, h, x, size, rows):
        for i in rows:
            for k in range(3):
                at = start(f, j + i, h) + x + k - 1
                total = total + weight(dwk_ref, 3 * i + k, h) * grid[pl.ds(at, size), :]
        return total

    def slot(f, j, h):
        return f * FACE_ROWS + (2 * j + h) * TURN + j + 8

    def inside(f, carry):
        for j in range(4):
            rows = (1, 2) if j == 0 else (0, 1) if j == 3 else (0, 1, 2)
            for h in range(2):
                for x in (8, 64):
                    zero = jnp.broadcast_to(weight(dwb_ref, 0, h), (56, LANES))
                    turned[pl.ds(slot(f, j, h) + x, 56), :] = partial_sum(
                        zero, f, j, h, x, 56, rows)
        return carry

    lax.fori_loop(0, 3, inside, 0)

    def took(ref, sem):
        push(ref, ref, row_sent.at[0, 0], sem, face, sub).wait_recv()

    for f in range(3):
        pl.when((sub > 0) if f == 2 else (sub >= 0))(
            lambda f=f: took(row_lo.at[f], lo_sem.at[f]))
        pl.when((sub < 31) if f == 0 else (sub >= 0))(
            lambda f=f: took(row_hi.at[f], hi_sem.at[f]))
    took(right0, piece_sem.at[0])
    took(left2, piece_sem.at[1])
    for e, cond in ((0, sub > 0), (1, sub >= 0), (2, sub < 31)):
        pl.when(cond)(lambda e=e: took(left1.at[e], left_sem.at[e]))
        pl.when(cond)(lambda e=e: took(right2.at[e], right_sem.at[e]))

    for f in range(3):
        for h in range(2):
            half = slice(h * LANES, (h + 1) * LANES)
            grid[pl.ds(start(f, 0, h), SIDE), :] = row_lo[f, :, half].astype(jnp.float32)
            grid[pl.ds(start(f, 5, h), SIDE), :] = row_hi[f, :, half].astype(jnp.float32)

    def rim(ref, sem, f, r):
        took(ref, sem)
        rim_rows[...] = ref[...].astype(jnp.float32).reshape(2 * SIDE, LANES)
        for h in range(2):
            grid[pl.ds(start(f, r, h), SIDE), :] = rim_rows[pl.ds(h, SIDE, stride=2), :]

    pl.when(first)(lambda: rim(rim_lo, rim_sem.at[1], 2, 0))
    pl.when(last)(lambda: rim(rim_hi, rim_sem.at[0], 0, 5))

    for r, size in ((0, 8), (4, 4)):
        grid[pl.ds(start(0, r) - 1, size, stride=PITCH), :] = grid[
            pl.ds(start(1, r) + SIDE - 1, size, stride=PITCH), :]
        grid[pl.ds(start(1, r) + SIDE, size, stride=PITCH), :] = grid[
            pl.ds(start(0, r), size, stride=PITCH), :]
    for f, x, ref in ((1, -1, left1), (2, SIDE, right2)):
        before = ref[0].astype(jnp.float32)
        after = ref[2].astype(jnp.float32)
        grid[pl.ds(start(f, 0) + x, 2, stride=PITCH), :] = before[6:8]
        grid[pl.ds(start(f, 1) + x, 8, stride=PITCH), :] = ref[1].astype(jnp.float32)
        grid[pl.ds(start(f, 5) + x, 2, stride=PITCH), :] = after[0:2]
    for f, x, ref in ((0, SIDE, right0), (2, -1, left2)):
        for h in range(2):
            grid[pl.ds(start(f, 0, h) + x, 6, stride=2 * PITCH), :] = ref[h].astype(jnp.float32)[:6]

    def corners(r):
        for f in range(3):
            for x in (-1, SIDE):
                grid[pl.ds(start(f, r) + x, 2, stride=PITCH), :] = jnp.zeros((2, LANES), jnp.float32)

    pl.when(first)(lambda: corners(0))
    pl.when(last)(lambda: corners(5))

    def around(f, carry):
        for j in range(4):
            for h in range(2):
                for x in (0, SIDE - 8):
                    zero = jnp.broadcast_to(weight(dwb_ref, 0, h), (8, LANES))
                    turned[pl.ds(slot(f, j, h) + x, 8), :] = partial_sum(
                        zero, f, j, h, x, 8, (0, 1, 2))
                if j in (0, 3):
                    for x in (8, 64):
                        at = pl.ds(slot(f, j, h) + x, 56)
                        turned[at, :] = partial_sum(
                            turned[at, :], f, j, h, x, 56, (0,) if j == 0 else (2,))
                if j:
                    turned[pl.ds(slot(f, j, h) - j, j), :] = turned[
                        pl.ds(slot(f, j, h) + SIDE - j, j), :]
        return carry

    lax.fori_loop(0, 3, around, 0)

    def pack(pf, ps):
        c = pf * 32 + ps
        t = (c - 4 * sub) & (ALL - 1)
        for f in range(3):
            cells = turned[pl.ds(f * FACE_ROWS + 8 + t, 8, stride=TURN), :]
            send[c, f] = cells.astype(jnp.bfloat16)

    exchange(face, sub, pack, send, recv, send_sem.at[3], recv_sem.at[3])
    pack(face, sub)
    recv[me] = send[me]
    settle(face, sub, send, recv, send_sem.at[3], recv_sem.at[3])
    for cond, copy in inner:
        pl.when(cond)(copy.wait_send)
    pl.when(first | last)(
        lambda: push(pieces, pieces, piece_sent, piece_sem.at[0], face, sub).wait_send())

    c = me
    row_in = lax.broadcasted_iota(jnp.int32, (8, LANES), 0) // 2

    def unpack(i, carry):
        q = i >> 5
        s = i & 31
        at = (3 - q) * 32 + s
        upper = row_in + 4 * s > c
        north = recv[i, 0].astype(jnp.float32)
        middle = recv[i, 1].astype(jnp.float32)
        south = recv[i, 2].astype(jnp.float32)
        chain1[at + 3] = jnp.where(upper, middle, north)
        before = recv[(i + 96) & (ALL - 1), 2].astype(jnp.float32)
        chain2[at + 3] = jnp.where(upper, before, middle)
        polar[pl.ds(pl.multiple_of(8 * i, 8), 8), :] = jnp.where(upper, north, south)
        return carry

    lax.fori_loop(0, ALL, unpack, 0, unroll=4)
    for chain in (chain1, chain2):
        for e in range(3):
            chain[e] = chain[ALL + e]
            chain[ALL + 3 + e] = chain[3 + e]

    def coeff(ref, k):
        lo = jnp.broadcast_to(ref[k : k + 1, :LANES], (8, LANES))
        hi = jnp.broadcast_to(ref[k : k + 1, LANES:], (8, LANES))
        odd = lax.rem(lax.broadcasted_iota(jnp.int32, (8, LANES), 0), 2) == 1
        return jnp.where(odd, hi, lo)

    taps = [coeff(zk_ref, k) for k in range(TAPS)]
    bias = coeff(zb_ref, 0)

    def middle(pf, ps):
        at = (3 - pf) * 32 + ps
        i = pf * 32 + ps
        upper = row_in + 4 * ps > c
        z1 = bias
        z2 = bias
        for k in range(TAPS):
            z1 = z1 + taps[k] * chain1[at + 6 - k]
            z2 = z2 + taps[k] * chain2[at + 6 - k]
        back_send[1, i] = jnp.where(upper, z1, z2).astype(jnp.bfloat16)
        back_send[0, i] = z1.astype(jnp.bfloat16)
        back_send[2, (i + 96) & (ALL - 1)] = z2.astype(jnp.bfloat16)

    exchange(face, sub, middle, back_send.at[1], back_recv.at[1], send_sem.at[1], recv_sem.at[1])
    middle(face, sub)
    back_recv[1, me] = back_send[1, me]

    arc_n = SIDE - 1 - c
    arc_s = c + 1
    base_s = BASE_N + 8 * arc_n + 48
    for q in range(4):
        lin[pl.ds(BASE_N + (3 - q) * 2 * arc_n - 2 * (c + 1), 256), :] = polar[
            q * 256 : (q + 1) * 256, :
        ]
    for q in (3, 2, 1, 0):
        lin[pl.ds(base_s + (3 - q) * 2 * arc_s, 256), :] = polar[q * 256 : (q + 1) * 256, :]
    for base, size in ((BASE_N, 8 * arc_n), (base_s, 8 * arc_s)):
        for e in range(3):
            lin[pl.ds(base + size + 8 * e, 8), :] = lin[pl.ds(base + 8 * e, 8), :]
        for e in range(1, 4):
            lin[pl.ds(base - 8 * e, 8), :] = lin[pl.ds(base - 8 * e + size, 8), :]

    def stencil_lin(v, carry):
        at = pl.multiple_of(BASE_N + 8 * v, 8)
        total = bias
        for k in range(TAPS):
            total = total + taps[k] * lin[pl.ds(pl.multiple_of(at - 8 * (k - 3), 8), 8), :]
        zlin[pl.ds(at, 8), :] = total
        return carry

    lax.fori_loop(0, ZROWS // 8, stencil_lin, 0, unroll=2)
    row_256 = lax.broadcasted_iota(jnp.int32, (256, LANES), 0) // 2
    for q in range(4):
        from_n = zlin[pl.ds(BASE_N + (3 - q) * 2 * arc_n - 2 * (c + 1), 256), :]
        from_s = zlin[pl.ds(base_s + (3 - q) * 2 * arc_s, 256), :]
        polar[q * 256 : (q + 1) * 256, :] = jnp.where(row_256 > c, from_n, from_s)

    def ends(f):
        def one(pf, ps):
            i = pf * 32 + ps
            upper = row_in + 4 * ps > c
            zp = polar[pl.ds(pl.multiple_of(8 * i, 8), 8), :]
            zm = back_send[f, i].astype(jnp.float32)
            back_send[f, i] = jnp.where(upper == (f == 0), zp, zm).astype(jnp.bfloat16)

        exchange(face, sub, one, back_send.at[f], back_recv.at[f], send_sem.at[f], recv_sem.at[f])
        one(face, sub)
        back_recv[f, me] = back_send[f, me]

    ends(0)
    ends(2)

    def unturn(f):
        def one(i, carry):
            t = (i - 4 * sub) & (ALL - 1)
            turned[pl.ds(f * FACE_ROWS + 8 + t, 8, stride=TURN), :] = back_recv[f, i].astype(
                jnp.float32)
            return carry

        lax.fori_loop(0, ALL, one, 0, unroll=8)
        for j in range(1, 4):
            for h in range(2):
                turned[pl.ds(slot(f, j, h) + SIDE - j, j), :] = turned[
                    pl.ds(slot(f, j, h) - j, j), :]

    gain = gain_ref[...]
    scale = ls_ref[...]
    w_in = w_in_ref[...]
    w_out = w_out_ref[...]

    def mlp(f, j, carry):
        base = f * FACE_ROWS + 2 * j * TURN + j + 8
        values = jnp.concatenate(
            [turned[pl.ds(base, SIDE), :], turned[pl.ds(base + TURN, SIDE), :]], axis=1
        )
        mean = jnp.mean(values, -1, keepdims=True)
        centred = values - mean
        spread = jnp.mean(jnp.square(centred), -1, keepdims=True)
        normed = (centred * lax.rsqrt(spread + 1e-06) * gain).astype(jnp.bfloat16)
        pre = jnp.dot(normed, w_in, preferred_element_type=jnp.float32)
        hidden = (0.5 * pre * (1.0 + lax.erf(pre * np.float32(np.sqrt(0.5))))).astype(jnp.bfloat16)
        branch = jnp.dot(hidden, w_out, preferred_element_type=jnp.float32)
        result = field_ref[f, j].astype(jnp.float32) + scale * branch
        out_ref[f, j] = result.astype(jnp.bfloat16)
        return carry

    for f in (1, 0, 2):
        settle(face, sub, back_send.at[f], back_recv.at[f], send_sem.at[f], recv_sem.at[f])
        unturn(f)
        lax.fori_loop(0, 4, functools.partial(mlp, f), 0)


def run(field, dw_kernel, dw_bias, zonal_kernel, zonal_bias, norm_gain, w_in, w_out, layer_scale):
    vmem = pl.BlockSpec(memory_space=pltpu.VMEM)
    cells = pltpu.VMEM((ALL, 3, 8, LANES), jnp.bfloat16)
    lines = pltpu.VMEM((3, SIDE, 2 * LANES), jnp.bfloat16)
    tiles = lambda *lead: pltpu.VMEM((*lead, 8, LANES), jnp.bfloat16)
    rows = lambda n: pltpu.VMEM((n, LANES), jnp.float32)
    vector = pltpu.VMEM((1, 2 * LANES), jnp.float32)
    back = pltpu.VMEM((3, ALL, 8, LANES), jnp.bfloat16)
    dma = pltpu.SemaphoreType.DMA
    return pl.pallas_call(
        kernel,
        out_shape=jax.ShapeDtypeStruct(field.shape, jnp.bfloat16),
        in_specs=[pl.BlockSpec(memory_space=pltpu.HBM)] * 9,
        out_specs=vmem,
        scratch_shapes=[
            pltpu.VMEM(field.shape, field.dtype),
            pltpu.VMEM(dw_kernel.shape, jnp.float32),
            vector,
            pltpu.VMEM(zonal_kernel.shape, jnp.float32),
            vector,
            vector,
            pltpu.VMEM(w_in.shape, w_in.dtype),
            pltpu.VMEM(w_out.shape, w_out.dtype),
            vector,
            dma((9,)),
            rows(36 * PITCH + 16),
            lines,
            lines,
            tiles(4),
            tiles(3),
            tiles(3),
            tiles(32, 2),
            tiles(2),
            tiles(2),
            tiles(32),
            tiles(32),
            rows(2 * SIDE),
            rows(3 * FACE_ROWS + 8),
            cells,
            cells,
            pltpu.VMEM((ALL + 6, 8, LANES), jnp.float32),
            pltpu.VMEM((ALL + 6, 8, LANES), jnp.float32),
            rows(1024),
            rows(LIN_ROWS),
            rows(LIN_ROWS),
            back,
            back,
            dma((4,)),
            dma((4,)),
            dma((2, 3)),
            dma((3,)),
            dma((3,)),
            dma((2, 3)),
            dma((3,)),
            dma((3,)),
            dma,
            dma((2,)),
            dma((2,)),
            dma((2,)),
        ],
        compiler_params=pltpu.CompilerParams(
            collective_id=0, has_side_effects=True, vmem_limit_bytes=24 * 1024 * 1024
        ),
    )(*[pltpu.with_memory_space_constraint(a, pltpu.HBM) for a in (
        field, dw_kernel, dw_bias[None], zonal_kernel, zonal_bias[None], norm_gain[None], w_in,
        w_out, layer_scale[None],
    )])


def shards(
    field, dw_kernel, dw_bias, zonal_kernel, zonal_bias, norm_gain, w_in, w_out, layer_scale
):
    output = run(
        field[:, 0], dw_kernel, dw_bias, zonal_kernel, zonal_bias, norm_gain, w_in, w_out,
        layer_scale,
    )
    return output[:, None]


def solution(mesh):
    in_specs = (P(None, "face", "sub", None, None), P(), P(), P(), P(), P(), P(), P(), P())
    out_specs = P(None, "face", "sub", None, None)
    return jax.shard_map(shards, mesh=mesh, in_specs=in_specs, out_specs=out_specs, check_vma=False)
```

```python
import functools

import jax
import jax.numpy as jnp
import numpy as np
from jax import lax
from jax.experimental import pallas as pl
from jax.experimental.pallas import tpu as pltpu
from jax.sharding import PartitionSpec as P

MESH = pl.DeviceIdType.MESH
TAPS = 7
SIDE = 128
ALL = 128
LANES = 128
PITCH = 137
ROW = 8
TURN = 137
FACE_ROWS = 8 * TURN + 16
BASE_N = 288
LIN_ROWS = 1664
LIN_BLOCKS = 17


def peer_at(face, sub, step):
    pf = (face + step) & 3
    px = ((sub >> 3) + (step >> 2)) & 3
    pz = ((sub >> 1) + (step >> 4)) & 3
    pc = (sub + (step >> 6)) & 1
    return pf, (px << 3) + (pz << 1) + pc


def announce(face, sub):
    barrier = pltpu.get_barrier_semaphore()

    def greet(i, carry):
        pf, ps = peer_at(face, sub, ALL - i)
        pl.semaphore_signal(barrier, inc=1, device_id=(pf, ps), device_id_type=MESH)
        return carry

    lax.fori_loop(1, ALL, greet, 0, unroll=2)


def exchange(face, sub, prepare, source, target, send_sem, recv_sem):
    me = face * 32 + sub

    def push(pf, ps):
        pltpu.make_async_remote_copy(
            source.at[pf * 32 + ps],
            target.at[me],
            send_sem,
            recv_sem,
            device_id=(pf, ps),
            device_id_type=MESH,
        ).start()

    def step(i, carry):
        pf, ps = peer_at(face, sub, ALL - i)
        prepare(pf, ps)
        push(*carry)
        return pf, ps

    pf, ps = peer_at(face, sub, ALL - 1)
    prepare(pf, ps)
    push(*lax.fori_loop(2, ALL, step, (pf, ps), unroll=2))


def dispatch(face, sub, source, target, send_sem, recv_sem):
    me = face * 32 + sub

    def step(i, carry):
        pf, ps = peer_at(face, sub, ALL - i)
        pltpu.make_async_remote_copy(
            source.at[pf * 32 + ps],
            target.at[me],
            send_sem,
            recv_sem,
            device_id=(pf, ps),
            device_id_type=MESH,
        ).start()
        return carry

    lax.fori_loop(1, ALL, step, 0, unroll=2)


def all_blocks(face, sub, source, target, send_sem, recv_sem):
    return pltpu.make_async_remote_copy(
        source.at[pl.ds(0, ALL - 1)],
        target.at[pl.ds(0, ALL - 1)],
        send_sem,
        recv_sem,
        device_id=(face, sub),
        device_id_type=MESH,
    )


def kernel(
    field_hbm, dwk_hbm, dwb_hbm, zk_hbm, zb_hbm, gain_hbm, w_in_hbm, w_out_hbm, ls_hbm, out_ref,
    field_ref, dwk_ref, dwb_ref, zk_ref, zb_ref, gain_ref, w_in_ref, w_out_ref, ls_ref, load_sem,
    grid, row_lo, row_hi, cols, left1, right2, pieces, right0, left2, rim_hi, rim_lo, rim_rows,
    turned, send, recv, chain, ring, polar, lin, zlin, back_send, back_recv,
    send_sem, recv_sem, row_sent, lo_sem, hi_sem, col_sent, left_sem, right_sem, piece_sent,
    piece_sem, rim_sent, rim_sem,
):
    face = lax.axis_index("face")
    sub = lax.axis_index("sub")
    me = face * 32 + sub
    east = (face + 1) & 3
    west = (face + 3) & 3
    first = sub == 0
    last = sub == 31
    loads = [
        pltpu.make_async_copy(source, target, load_sem.at[n])
        for n, (source, target) in enumerate((
            (field_hbm, field_ref), (dwk_hbm, dwk_ref), (dwb_hbm, dwb_ref), (zk_hbm, zk_ref),
            (zb_hbm, zb_ref), (gain_hbm, gain_ref), (w_in_hbm, w_in_ref), (w_out_hbm, w_out_ref),
            (ls_hbm, ls_ref)))
    ]
    loads[0].start()
    announce(face, sub)
    for load in loads[1:]:
        load.start()
    loads[0].wait()

    def start(f, r, h=0):
        return (f * 12 + r * 2 + h) * PITCH + ROW

    def widen(t, carry):
        f = t >> 2
        j = t & 3
        for h in range(2):
            grid[pl.ds(start(f, j + 1, h), SIDE), :] = field_ref[
                f, j, :, h * LANES : (h + 1) * LANES
            ].astype(jnp.float32)
        return carry

    lax.fori_loop(0, 12, widen, 0)
    for n, (f, x) in enumerate(((2, SIDE - 1), (1, 0), (0, SIDE - 1), (2, 0))):
        cols[n] = grid[pl.ds(start(f, 1) + x, 8, stride=PITCH), :].astype(jnp.bfloat16)

    def cut(base):
        def one(t, carry):
            for h in range(2):
                at = base + h * PITCH + 4 * t - 1
                pieces[t, h] = grid[pl.ds(at, 8), :].astype(jnp.bfloat16)
            return carry

        lax.fori_loop(0, 32, one, 0)

    pl.when(last)(lambda: cut(start(0, 4)))
    pl.when(first)(lambda: cut(start(2, 1)))

    def push(source, target, sent, got, pf, ps):
        return pltpu.make_async_remote_copy(
            source, target, sent, got, device_id=(pf, ps), device_id_type=MESH
        )

    inner = []
    for f in range(3):
        inner.append((sub < 31, push(
            field_ref.at[f, 3], row_lo.at[f], row_sent.at[0, f], lo_sem.at[f], face, sub + 1)))
        inner.append((sub > 0, push(
            field_ref.at[f, 0], row_hi.at[f], row_sent.at[1, f], hi_sem.at[f], face, sub - 1)))
    inner.append((last, push(
        field_ref.at[1, 3], row_lo.at[0], row_sent.at[0, 1], lo_sem.at[0], west, 0)))
    inner.append((last, push(
        field_ref.at[2, 3], row_lo.at[1], row_sent.at[0, 2], lo_sem.at[1], face, 0)))
    inner.append((first, push(
        field_ref.at[0, 0], row_hi.at[1], row_sent.at[1, 0], hi_sem.at[1], east, 31)))
    inner.append((first, push(
        field_ref.at[1, 0], row_hi.at[2], row_sent.at[1, 1], hi_sem.at[2], face, 31)))
    for d, cond in ((-1, sub > 0), (0, sub >= 0), (1, sub < 31)):
        inner.append((cond, push(
            cols.at[0], left1.at[1 - d], col_sent.at[0, 1 - d], left_sem.at[1 - d], east, sub + d)))
        inner.append((cond, push(
            cols.at[1], right2.at[1 - d], col_sent.at[1, 1 - d], right_sem.at[1 - d], west, sub + d)))
    inner.append((sub >= 0, push(
        cols.at[2], rim_hi.at[sub], rim_sent.at[0], rim_sem.at[0], east, 31)))
    inner.append((sub >= 0, push(
        cols.at[3], rim_lo.at[sub], rim_sent.at[1], rim_sem.at[1], west, 0)))

    pl.semaphore_wait(pltpu.get_barrier_semaphore(), ALL - 1)
    for cond, copy in inner:
        pl.when(cond)(copy.start)

    def scatter(pf, target, got):
        def one(t, carry):
            push(pieces.at[t], target, piece_sent, got, pf, t).start()
            return carry

        lax.fori_loop(0, 32, one, 0)

    pl.when(last)(lambda: scatter(west, right0, piece_sem.at[0]))
    pl.when(first)(lambda: scatter(east, left2, piece_sem.at[1]))

    for load in loads[1:]:
        load.wait()

    def weight(ref, tap, h):
        return ref[tap : tap + 1, h * LANES : (h + 1) * LANES]

    def partial_sum(total, f, j, h, x, size, rows):
        for i in rows:
            for k in range(3):
                at = start(f, j + i, h) + x + k - 1
                total = total + weight(dwk_ref, 3 * i + k, h) * grid[pl.ds(at, size), :]
        return total

    def slot(f, j, h):
        return f * FACE_ROWS + (2 * j + h) * TURN + j + 8

    def inside(f, carry):
        for j in range(4):
            rows = (1, 2) if j == 0 else (0, 1) if j == 3 else (0, 1, 2)
            for h in range(2):
                for x in (8, 64):
                    zero = jnp.broadcast_to(weight(dwb_ref, 0, h), (56, LANES))
                    turned[pl.ds(slot(f, j, h) + x, 56), :] = partial_sum(
                        zero, f, j, h, x, 56, rows)
        return carry

    lax.fori_loop(0, 3, inside, 0)

    def took(ref, sem):
        push(ref, ref, row_sent.at[0, 0], sem, face, sub).wait_recv()

    for f in range(3):
        pl.when((sub > 0) if f == 2 else (sub >= 0))(
            lambda f=f: took(row_lo.at[f], lo_sem.at[f]))
        pl.when((sub < 31) if f == 0 else (sub >= 0))(
            lambda f=f: took(row_hi.at[f], hi_sem.at[f]))
    took(right0, piece_sem.at[0])
    took(left2, piece_sem.at[1])
    for e, cond in ((0, sub > 0), (1, sub >= 0), (2, sub < 31)):
        pl.when(cond)(lambda e=e: took(left1.at[e], left_sem.at[e]))
        pl.when(cond)(lambda e=e: took(right2.at[e], right_sem.at[e]))

    for f in range(3):
        for h in range(2):
            half = slice(h * LANES, (h + 1) * LANES)
            grid[pl.ds(start(f, 0, h), SIDE), :] = row_lo[f, :, half].astype(jnp.float32)
            grid[pl.ds(start(f, 5, h), SIDE), :] = row_hi[f, :, half].astype(jnp.float32)

    def rim(ref, sem, f, r):
        took(ref, sem)
        rim_rows[...] = ref[...].astype(jnp.float32).reshape(2 * SIDE, LANES)
        for h in range(2):
            grid[pl.ds(start(f, r, h), SIDE), :] = rim_rows[pl.ds(h, SIDE, stride=2), :]

    pl.when(first)(lambda: rim(rim_lo, rim_sem.at[1], 2, 0))
    pl.when(last)(lambda: rim(rim_hi, rim_sem.at[0], 0, 5))

    for r, size in ((0, 8), (4, 4)):
        grid[pl.ds(start(0, r) - 1, size, stride=PITCH), :] = grid[
            pl.ds(start(1, r) + SIDE - 1, size, stride=PITCH), :]
        grid[pl.ds(start(1, r) + SIDE, size, stride=PITCH), :] = grid[
            pl.ds(start(0, r), size, stride=PITCH), :]
    for f, x, ref in ((1, -1, left1), (2, SIDE, right2)):
        before = ref[0].astype(jnp.float32)
        after = ref[2].astype(jnp.float32)
        grid[pl.ds(start(f, 0) + x, 2, stride=PITCH), :] = before[6:8]
        grid[pl.ds(start(f, 1) + x, 8, stride=PITCH), :] = ref[1].astype(jnp.float32)
        grid[pl.ds(start(f, 5) + x, 2, stride=PITCH), :] = after[0:2]
    for f, x, ref in ((0, SIDE, right0), (2, -1, left2)):
        for h in range(2):
            grid[pl.ds(start(f, 0, h) + x, 6, stride=2 * PITCH), :] = ref[h].astype(jnp.float32)[:6]

    def corners(r):
        for f in range(3):
            for x in (-1, SIDE):
                grid[pl.ds(start(f, r) + x, 2, stride=PITCH), :] = jnp.zeros((2, LANES), jnp.float32)

    pl.when(first)(lambda: corners(0))
    pl.when(last)(lambda: corners(5))

    def around(f, carry):
        for j in range(4):
            for h in range(2):
                for x in (0, SIDE - 8):
                    zero = jnp.broadcast_to(weight(dwb_ref, 0, h), (8, LANES))
                    turned[pl.ds(slot(f, j, h) + x, 8), :] = partial_sum(
                        zero, f, j, h, x, 8, (0, 1, 2))
                if j in (0, 3):
                    for x in (8, 64):
                        at = pl.ds(slot(f, j, h) + x, 56)
                        turned[at, :] = partial_sum(
                            turned[at, :], f, j, h, x, 56, (0,) if j == 0 else (2,))
                if j:
                    turned[pl.ds(slot(f, j, h) - j, j), :] = turned[
                        pl.ds(slot(f, j, h) + SIDE - j, j), :]
        return carry

    lax.fori_loop(0, 3, around, 0)

    high = (0, 1, 2)
    low = (2, 0, 1)
    row_in = lax.broadcasted_iota(jnp.int32, (8, LANES), 0) // 2
    for g in range(3):

        def pack(pf, ps, g=g):
            c = pf * 32 + ps
            t = (c - 4 * sub) & (ALL - 1)
            above = turned[pl.ds(high[g] * FACE_ROWS + 8 + t, 8, stride=TURN), :]
            below = turned[pl.ds(low[g] * FACE_ROWS + 8 + t, 8, stride=TURN), :]
            send[g, c] = jnp.where(row_in + 4 * sub > c, above, below).astype(jnp.bfloat16)

        exchange(face, sub, pack, send.at[g], recv.at[g], send_sem.at[g], recv_sem.at[g])
        pack(face, sub)
        recv[g, me] = send[g, me]

    c = me
    def coeff(ref, k):
        lo = jnp.broadcast_to(ref[k : k + 1, :LANES], (8, LANES))
        hi = jnp.broadcast_to(ref[k : k + 1, LANES:], (8, LANES))
        odd = lax.rem(lax.broadcasted_iota(jnp.int32, (8, LANES), 0), 2) == 1
        return jnp.where(odd, hi, lo)

    taps = [coeff(zk_ref, k) for k in range(TAPS)]
    bias = coeff(zb_ref, 0)

    def blend(terms):
        products = [tap * term for tap, term in zip(taps, terms)]
        return ((products[0] + products[1]) + (products[2] + products[3])) + (
            (products[4] + products[5]) + (products[6] + bias))

    def arrive(g):
        all_blocks(face, sub, send.at[g], recv.at[g], send_sem.at[g], recv_sem.at[g]).wait_recv()

    def depart(g):
        back_recv[g, me] = back_send[g, me]
        dispatch(
            face, sub, back_send.at[g], back_recv.at[g], send_sem.at[3 + g], recv_sem.at[3 + g])

    arrive(0)

    def lay(b, carry):
        rows = recv[0, pl.ds(8 * b, 8)].astype(jnp.float32)
        polar[pl.ds(pl.multiple_of(64 * b, 64), 64), :] = rows.reshape(64, LANES)
        return carry

    lax.fori_loop(0, 16, lay, 0, unroll=2)
    arc_n = SIDE - 1 - c
    arc_s = c + 1
    base_s = BASE_N + 8 * arc_n + 48
    for q in range(4):
        lin[pl.ds(BASE_N + (3 - q) * 2 * arc_n - 2 * (c + 1), 256), :] = polar[
            q * 256 : (q + 1) * 256, :
        ]
    for q in (3, 2, 1, 0):
        lin[pl.ds(base_s + (3 - q) * 2 * arc_s, 256), :] = polar[q * 256 : (q + 1) * 256, :]
    for base, size in ((BASE_N, 8 * arc_n), (base_s, 8 * arc_s)):
        for e in range(3):
            lin[pl.ds(base + size + 8 * e, 8), :] = lin[pl.ds(base + 8 * e, 8), :]
        for e in range(1, 4):
            lin[pl.ds(base - 8 * e, 8), :] = lin[pl.ds(base - 8 * e + size, 8), :]


    def stencil_lin(v, carry):
        at = pl.multiple_of(BASE_N + 64 * v, 8)
        window = [lin[pl.ds(pl.multiple_of(at + 8 * (n - 3), 8), 8), :] for n in range(14)]
        for n in range(8):
            zlin[pl.ds(pl.multiple_of(at + 8 * n, 8), 8), :] = blend(window[n : n + 7][::-1])
        return carry

    lax.fori_loop(0, LIN_BLOCKS, stencil_lin, 0)
    row_256 = lax.broadcasted_iota(jnp.int32, (256, LANES), 0) // 2
    for q in range(4):
        from_n = zlin[pl.ds(BASE_N + (3 - q) * 2 * arc_n - 2 * (c + 1), 256), :]
        from_s = zlin[pl.ds(base_s + (3 - q) * 2 * arc_s, 256), :]
        back_send[0, pl.ds(32 * q, 32)] = (
            jnp.where(row_256 > c, from_n, from_s).reshape(32, 8, LANES).astype(jnp.bfloat16))
    depart(0)

    block_row = 4 * lax.broadcasted_iota(jnp.int32, (8, 8, LANES), 0) + (
        lax.broadcasted_iota(jnp.int32, (8, 8, LANES), 1) // 2)

    for g in (1, 2):
        arrive(g)

        def unpack(b, carry, g=g):
            at = pl.multiple_of(8 * b, 8)
            i = (3 - (b >> 2)) * 32 + 8 * (b & 3)
            rows = recv[g, pl.ds(i, 8)].astype(jnp.float32)
            if g == 2:
                before = recv[g, pl.ds((i + 96) & (ALL - 1), 8)].astype(jnp.float32)
                rows = jnp.where(block_row + 32 * (b & 3) > c, before, rows)
            chain[pl.ds(at + 3, 8)] = rows
            return carry

        lax.fori_loop(0, 16, unpack, 0, unroll=2)
        for e in range(3):
            chain[e] = chain[ALL + e]
            chain[ALL + 3 + e] = chain[3 + e]

        def stencil_ring(b, carry, g=g):
            at = 8 * b
            i = (3 - (b >> 2)) * 32 + 8 * (b & 3)
            window = [chain[at + n] for n in range(14)]
            for n in range(8):
                total = blend(window[n : n + 7][::-1])
                if g == 1:
                    back_send[g, i + n] = total.astype(jnp.bfloat16)
                else:
                    ring[i + n] = total
            return carry

        lax.fori_loop(0, 16, stencil_ring, 0)
        if g == 2:

            def regroup(b, carry):
                rows = ring[pl.ds(8 * b, 8)]
                after = ring[pl.ds((8 * b + 32) & (ALL - 1), 8)]
                back_send[2, pl.ds(8 * b, 8)] = jnp.where(
                    block_row + 32 * (b & 3) > c, after, rows).astype(jnp.bfloat16)
                return carry

            lax.fori_loop(0, 16, regroup, 0, unroll=2)
        depart(g)

    gain = gain_ref[...]
    scale = ls_ref[...]
    w_in = w_in_ref[...]
    w_out = w_out_ref[...]
    column = lax.broadcasted_iota(jnp.int32, (SIDE, 2 * LANES), 0)

    def mlp(g, j, carry):
        base = g * FACE_ROWS + 2 * j * TURN + j + 8
        values = jnp.concatenate(
            [turned[pl.ds(base, SIDE), :], turned[pl.ds(base + TURN, SIDE), :]], axis=1
        )
        mean = jnp.mean(values, -1, keepdims=True)
        centred = values - mean
        spread = jnp.mean(jnp.square(centred), -1, keepdims=True)
        normed = (centred * lax.rsqrt(spread + 1e-06) * gain).astype(jnp.bfloat16)
        pre = jnp.dot(normed, w_in, preferred_element_type=jnp.float32)
        hidden = (0.5 * pre * (1.0 + lax.erf(pre * np.float32(np.sqrt(0.5))))).astype(jnp.bfloat16)
        branch = jnp.dot(hidden, w_out, preferred_element_type=jnp.float32)
        upper = column + 4 * sub + j >= SIDE
        source = jnp.where(
            upper, field_ref[high[g], j].astype(jnp.float32), field_ref[low[g], j].astype(jnp.float32))
        result = source + scale * branch
        for f, kept in ((high[g], upper), (low[g], jnp.logical_not(upper))):
            seen = (g, f) in ((1, 0), (2, 1), (2, 2))
            row = jnp.where(kept, result, out_ref[f, j].astype(jnp.float32)) if seen else result
            out_ref[f, j] = row.astype(jnp.bfloat16)
        return carry

    for g in range(3):
        all_blocks(
            face, sub, back_send.at[g], back_recv.at[g], send_sem.at[3 + g], recv_sem.at[3 + g]
        ).wait_recv()

        def unturn(i, carry, g=g):
            t = (i - 4 * sub) & (ALL - 1)
            turned[pl.ds(g * FACE_ROWS + 8 + t, 8, stride=TURN), :] = back_recv[g, i].astype(
                jnp.float32)
            return carry

        lax.fori_loop(0, ALL, unturn, 0, unroll=8)
        for j in range(1, 4):
            for h in range(2):
                turned[pl.ds(slot(g, j, h) + SIDE - j, j), :] = turned[
                    pl.ds(slot(g, j, h) - j, j), :]
        lax.fori_loop(0, 4, functools.partial(mlp, g), 0)

    for cond, copy in inner:
        pl.when(cond)(copy.wait_send)
    pl.when(first | last)(
        lambda: push(pieces, pieces, piece_sent, piece_sem.at[0], face, sub).wait_send())
    for g in range(3):
        all_blocks(face, sub, send.at[g], recv.at[g], send_sem.at[g], recv_sem.at[g]).wait_send()
        all_blocks(
            face, sub, back_send.at[g], back_recv.at[g], send_sem.at[3 + g], recv_sem.at[3 + g]
        ).wait_send()


def run(field, dw_kernel, dw_bias, zonal_kernel, zonal_bias, norm_gain, w_in, w_out, layer_scale):
    vmem = pl.BlockSpec(memory_space=pltpu.VMEM)
    lines = pltpu.VMEM((3, SIDE, 2 * LANES), jnp.bfloat16)
    tiles = lambda *lead: pltpu.VMEM((*lead, 8, LANES), jnp.bfloat16)
    rows = lambda n: pltpu.VMEM((n, LANES), jnp.float32)
    vector = pltpu.VMEM((1, 2 * LANES), jnp.float32)
    blocks = pltpu.VMEM((3, ALL, 8, LANES), jnp.bfloat16)
    dma = pltpu.SemaphoreType.DMA
    return pl.pallas_call(
        kernel,
        out_shape=jax.ShapeDtypeStruct(field.shape, jnp.bfloat16),
        in_specs=[pl.BlockSpec(memory_space=pltpu.HBM)] * 9,
        out_specs=vmem,
        scratch_shapes=[
            pltpu.VMEM(field.shape, field.dtype),
            pltpu.VMEM(dw_kernel.shape, jnp.float32),
            vector,
            pltpu.VMEM(zonal_kernel.shape, jnp.float32),
            vector,
            vector,
            pltpu.VMEM(w_in.shape, w_in.dtype),
            pltpu.VMEM(w_out.shape, w_out.dtype),
            vector,
            dma((9,)),
            rows(36 * PITCH + 16),
            lines,
            lines,
            tiles(4),
            tiles(3),
            tiles(3),
            tiles(32, 2),
            tiles(2),
            tiles(2),
            tiles(32),
            tiles(32),
            rows(2 * SIDE),
            rows(3 * FACE_ROWS + 8),
            blocks,
            blocks,
            pltpu.VMEM((ALL + 6, 8, LANES), jnp.float32),
            pltpu.VMEM((ALL, 8, LANES), jnp.float32),
            rows(1024),
            rows(LIN_ROWS),
            rows(LIN_ROWS),
            blocks,
            blocks,
            dma((6,)),
            dma((6,)),
            dma((2, 3)),
            dma((3,)),
            dma((3,)),
            dma((2, 3)),
            dma((3,)),
            dma((3,)),
            dma,
            dma((2,)),
            dma((2,)),
            dma((2,)),
        ],
        compiler_params=pltpu.CompilerParams(
            collective_id=0, has_side_effects=True, vmem_limit_bytes=24 * 1024 * 1024
        ),
    )(*[pltpu.with_memory_space_constraint(a, pltpu.HBM) for a in (
        field, dw_kernel, dw_bias[None], zonal_kernel, zonal_bias[None], norm_gain[None], w_in,
        w_out, layer_scale[None],
    )])


def shards(
    field, dw_kernel, dw_bias, zonal_kernel, zonal_bias, norm_gain, w_in, w_out, layer_scale
):
    output = run(
        field[:, 0], dw_kernel, dw_bias, zonal_kernel, zonal_bias, norm_gain, w_in, w_out,
        layer_scale,
    )
    return output[:, None]


def solution(mesh):
    in_specs = (P(None, "face", "sub", None, None), P(), P(), P(), P(), P(), P(), P(), P())
    out_specs = P(None, "face", "sub", None, None)
    return jax.shard_map(shards, mesh=mesh, in_specs=in_specs, out_specs=out_specs, check_vma=False)
```

```python
import functools

import jax
import jax.numpy as jnp
import numpy as np
from jax import lax
from jax.experimental import pallas as pl
from jax.experimental.pallas import tpu as pltpu
from jax.sharding import PartitionSpec as P

MESH = pl.DeviceIdType.MESH
TAPS = 7
SIDE = 128
ALL = 128
LANES = 128
PITCH = 137
ROW = 8
TURN = 137
FACE_ROWS = 8 * TURN + 16
BASE_N = 288
LIN_ROWS = 1664
LIN_BLOCKS = 17


def peer_at(face, sub, step):
    pf = (face + step) & 3
    px = ((sub >> 3) + (step >> 2)) & 3
    pz = ((sub >> 1) + (step >> 4)) & 3
    pc = (sub + (step >> 6)) & 1
    return pf, (px << 3) + (pz << 1) + pc


def greet(sem, pf, ps):
    pl.semaphore_signal(sem, inc=1, device_id=(pf, ps), device_id_type=MESH)


def announce(face, sub):
    barrier = pltpu.get_barrier_semaphore()
    east = (face + 1) & 3
    west = (face + 3) & 3
    for n in range(1, 8):
        greet(barrier, face, (sub & 24) + ((sub + n) & 7))
    for n in range(1, 4):
        greet(barrier, face, (sub + 8 * n) & 31)
        greet(barrier, (face + n) & 3, sub)
    edge = sub & 7
    for cond, pf, ps in (
        (sub > 0, east, sub - 1),
        (sub > 0, west, sub - 1),
        (sub < 31, east, sub + 1),
        (sub < 31, west, sub + 1),
        ((edge == 7) & (sub < 31), face, sub + 1),
        ((edge == 0) & (sub > 0), face, sub - 1),
        (sub == 31, face, 0),
        (sub == 31, west, 0),
        (sub == 0, face, 31),
        (sub == 0, east, 31),
    ):
        pl.when(cond)(functools.partial(greet, barrier, pf, ps))
    inner_edge = ((edge == 0) | (edge == 7)) & (sub > 0) & (sub < 31)
    return 17 + inner_edge.astype(jnp.int32)


def exchange(face, sub, prepare, source, target, send_sem, recv_sem, later=None):
    me = face * 32 + sub

    def push(pf, ps):
        copy = pltpu.make_async_remote_copy(
            source.at[pf * 32 + ps],
            target.at[me],
            send_sem,
            recv_sem,
            device_id=(pf, ps),
            device_id_type=MESH,
        )
        if later is None:
            copy.start()
        else:
            pl.when(pf * 32 + ps != later)(copy.start)

    def step(i, carry):
        pf, ps = peer_at(face, sub, ALL - i)
        prepare(pf, ps)
        push(*carry)
        return pf, ps

    pf, ps = peer_at(face, sub, ALL - 1)
    prepare(pf, ps)
    push(*lax.fori_loop(2, ALL, step, (pf, ps), unroll=2))


def dispatch(face, sub, source, target, send_sem, recv_sem):
    me = face * 32 + sub

    def step(i, carry):
        pf, ps = peer_at(face, sub, ALL - i)
        pltpu.make_async_remote_copy(
            source.at[pf * 32 + ps],
            target.at[me],
            send_sem,
            recv_sem,
            device_id=(pf, ps),
            device_id_type=MESH,
        ).start()
        return carry

    lax.fori_loop(1, ALL, step, 0, unroll=2)


def all_blocks(face, sub, source, target, send_sem, recv_sem):
    return pltpu.make_async_remote_copy(
        source.at[pl.ds(0, ALL - 1)],
        target.at[pl.ds(0, ALL - 1)],
        send_sem,
        recv_sem,
        device_id=(face, sub),
        device_id_type=MESH,
    )


def kernel(
    field_hbm, dwk_hbm, dwb_hbm, zk_hbm, zb_hbm, gain_hbm, w_in_hbm, w_out_hbm, ls_hbm, out_ref,
    field_ref, dwk_ref, dwb_ref, zk_ref, zb_ref, gain_ref, w_in_ref, w_out_ref, ls_ref, load_sem,
    grid, row_lo, row_hi, cols, left1, right2, pieces, right0, left2, rim_hi, rim_lo, rim_rows,
    turned, send, recv, chain, ring, polar, lin, zlin, back_send, back_recv,
    send_sem, recv_sem, round_sem, row_sent, lo_sem, hi_sem, col_sent, left_sem, right_sem, piece_sent,
    piece_sem, rim_sent, rim_sem,
):
    face = lax.axis_index("face")
    sub = lax.axis_index("sub")
    me = face * 32 + sub
    east = (face + 1) & 3
    west = (face + 3) & 3
    first = sub == 0
    last = sub == 31
    loads = [
        pltpu.make_async_copy(source, target, load_sem.at[n])
        for n, (source, target) in enumerate((
            (field_hbm, field_ref), (dwk_hbm, dwk_ref), (dwb_hbm, dwb_ref), (zk_hbm, zk_ref),
            (zb_hbm, zb_ref), (gain_hbm, gain_ref), (w_in_hbm, w_in_ref), (w_out_hbm, w_out_ref),
            (ls_hbm, ls_ref)))
    ]
    loads[0].start()
    partners = announce(face, sub)
    for load in loads[1:]:
        load.start()
    loads[0].wait()

    def start(f, r, h=0):
        return (f * 12 + r * 2 + h) * PITCH + ROW

    def widen(t, carry):
        f = t >> 2
        j = t & 3
        for h in range(2):
            grid[pl.ds(start(f, j + 1, h), SIDE), :] = field_ref[
                f, j, :, h * LANES : (h + 1) * LANES
            ].astype(jnp.float32)
        return carry

    lax.fori_loop(0, 12, widen, 0)
    for n, (f, x) in enumerate(((2, SIDE - 1), (1, 0), (0, SIDE - 1), (2, 0))):
        cols[n] = grid[pl.ds(start(f, 1) + x, 8, stride=PITCH), :].astype(jnp.bfloat16)

    def cut(base):
        def one(t, carry):
            for h in range(2):
                at = base + h * PITCH + 4 * t - 1
                pieces[t, h] = grid[pl.ds(at, 8), :].astype(jnp.bfloat16)
            return carry

        lax.fori_loop(0, 32, one, 0)

    pl.when(last)(lambda: cut(start(0, 4)))
    pl.when(first)(lambda: cut(start(2, 1)))

    def push(source, target, sent, got, pf, ps):
        return pltpu.make_async_remote_copy(
            source, target, sent, got, device_id=(pf, ps), device_id_type=MESH
        )

    inner = []
    for f in range(3):
        inner.append((sub < 31, push(
            field_ref.at[f, 3], row_lo.at[f], row_sent.at[0, f], lo_sem.at[f], face, sub + 1)))
        inner.append((sub > 0, push(
            field_ref.at[f, 0], row_hi.at[f], row_sent.at[1, f], hi_sem.at[f], face, sub - 1)))
    inner.append((last, push(
        field_ref.at[1, 3], row_lo.at[0], row_sent.at[0, 1], lo_sem.at[0], west, 0)))
    inner.append((last, push(
        field_ref.at[2, 3], row_lo.at[1], row_sent.at[0, 2], lo_sem.at[1], face, 0)))
    inner.append((first, push(
        field_ref.at[0, 0], row_hi.at[1], row_sent.at[1, 0], hi_sem.at[1], east, 31)))
    inner.append((first, push(
        field_ref.at[1, 0], row_hi.at[2], row_sent.at[1, 1], hi_sem.at[2], face, 31)))
    for d, cond in ((-1, sub > 0), (0, sub >= 0), (1, sub < 31)):
        inner.append((cond, push(
            cols.at[0], left1.at[1 - d], col_sent.at[0, 1 - d], left_sem.at[1 - d], east, sub + d)))
        inner.append((cond, push(
            cols.at[1], right2.at[1 - d], col_sent.at[1, 1 - d], right_sem.at[1 - d], west, sub + d)))
    outer = []
    outer.append(push(
        cols.at[2], rim_hi.at[sub], rim_sent.at[0], rim_sem.at[0], east, 31))
    outer.append(push(
        cols.at[3], rim_lo.at[sub], rim_sent.at[1], rim_sem.at[1], west, 0))

    pl.semaphore_wait(pltpu.get_barrier_semaphore(), partners)
    for cond, copy in inner:
        pl.when(cond)(copy.start)
    for n in range(1, 4):
        greet(round_sem.at[0], face, (sub + 8 * n) & 31)

    for load in loads[1:]:
        load.wait()

    def weight(ref, tap, h):
        return ref[tap : tap + 1, h * LANES : (h + 1) * LANES]

    def partial_sum(total, f, j, h, x, size, rows):
        for i in rows:
            for k in range(3):
                at = start(f, j + i, h) + x + k - 1
                total = total + weight(dwk_ref, 3 * i + k, h) * grid[pl.ds(at, size), :]
        return total

    def slot(f, j, h):
        return f * FACE_ROWS + (2 * j + h) * TURN + j + 8

    def inside(f, carry):
        for j in range(4):
            rows = (1, 2) if j == 0 else (0, 1) if j == 3 else (0, 1, 2)
            for h in range(2):
                for x in (8, 64):
                    zero = jnp.broadcast_to(weight(dwb_ref, 0, h), (56, LANES))
                    turned[pl.ds(slot(f, j, h) + x, 56), :] = partial_sum(
                        zero, f, j, h, x, 56, rows)
        return carry

    inside(0, 0)
    pl.semaphore_wait(round_sem.at[0], 3)
    for n in range(1, 4):
        greet(round_sem.at[1], (face + n) & 3, sub)
    lax.fori_loop(1, 3, inside, 0)
    pl.semaphore_wait(round_sem.at[1], 3)
    for copy in outer:
        copy.start()

    def scatter(pf, target, got):
        def one(t, carry):
            push(pieces.at[t], target, piece_sent, got, pf, t).start()
            return carry

        lax.fori_loop(0, 32, one, 0)

    pl.when(last)(lambda: scatter(west, right0, piece_sem.at[0]))
    pl.when(first)(lambda: scatter(east, left2, piece_sem.at[1]))

    def took(ref, sem):
        push(ref, ref, row_sent.at[0, 0], sem, face, sub).wait_recv()

    for f in range(3):
        pl.when((sub > 0) if f == 2 else (sub >= 0))(
            lambda f=f: took(row_lo.at[f], lo_sem.at[f]))
        pl.when((sub < 31) if f == 0 else (sub >= 0))(
            lambda f=f: took(row_hi.at[f], hi_sem.at[f]))
    for e, cond in ((0, sub > 0), (1, sub >= 0), (2, sub < 31)):
        pl.when(cond)(lambda e=e: took(left1.at[e], left_sem.at[e]))
        pl.when(cond)(lambda e=e: took(right2.at[e], right_sem.at[e]))

    for f in range(3):
        for h in range(2):
            half = slice(h * LANES, (h + 1) * LANES)
            grid[pl.ds(start(f, 0, h), SIDE), :] = row_lo[f, :, half].astype(jnp.float32)
            grid[pl.ds(start(f, 5, h), SIDE), :] = row_hi[f, :, half].astype(jnp.float32)

    for r, size in ((0, 8), (4, 4)):
        grid[pl.ds(start(0, r) - 1, size, stride=PITCH), :] = grid[
            pl.ds(start(1, r) + SIDE - 1, size, stride=PITCH), :]
        grid[pl.ds(start(1, r) + SIDE, size, stride=PITCH), :] = grid[
            pl.ds(start(0, r), size, stride=PITCH), :]
    for f, x, ref in ((1, -1, left1), (2, SIDE, right2)):
        before = ref[0].astype(jnp.float32)
        after = ref[2].astype(jnp.float32)
        grid[pl.ds(start(f, 0) + x, 2, stride=PITCH), :] = before[6:8]
        grid[pl.ds(start(f, 1) + x, 8, stride=PITCH), :] = ref[1].astype(jnp.float32)
        grid[pl.ds(start(f, 5) + x, 2, stride=PITCH), :] = after[0:2]
    def corners(r):
        for f in range(3):
            for x in (-1, SIDE):
                grid[pl.ds(start(f, r) + x, 2, stride=PITCH), :] = jnp.zeros((2, LANES), jnp.float32)

    pl.when(first)(lambda: corners(0))
    pl.when(last)(lambda: corners(5))

    def around(f, carry):
        for j in range(4):
            for h in range(2):
                for x in (0, SIDE - 8):
                    zero = jnp.broadcast_to(weight(dwb_ref, 0, h), (8, LANES))
                    turned[pl.ds(slot(f, j, h) + x, 8), :] = partial_sum(
                        zero, f, j, h, x, 8, (0, 1, 2))
                if j in (0, 3):
                    for x in (8, 64):
                        at = pl.ds(slot(f, j, h) + x, 56)
                        turned[at, :] = partial_sum(
                            turned[at, :], f, j, h, x, 56, (0,) if j == 0 else (2,))
                if j:
                    turned[pl.ds(slot(f, j, h) - j, j), :] = turned[
                        pl.ds(slot(f, j, h) + SIDE - j, j), :]
        return carry

    lax.fori_loop(0, 3, around, 0)

    high = (0, 1, 2)
    low = (2, 0, 1)
    row_in = lax.broadcasted_iota(jnp.int32, (8, LANES), 0) // 2

    def send_family(g, later=None):
        def pack(pf, ps):
            c = pf * 32 + ps
            t = (c - 4 * sub) & (ALL - 1)
            above = turned[pl.ds(high[g] * FACE_ROWS + 8 + t, 8, stride=TURN), :]
            below = turned[pl.ds(low[g] * FACE_ROWS + 8 + t, 8, stride=TURN), :]
            send[g, c] = jnp.where(row_in + 4 * sub > c, above, below).astype(jnp.bfloat16)

        exchange(
            face, sub, pack, send.at[g], recv.at[g], send_sem.at[g], recv_sem.at[g], later)
        pack(face, sub)
        recv[g, me] = send[g, me]
        return pack

    send_family(2)
    pack_1 = send_family(1, ALL - 1)

    def rim(ref, sem, f, r):
        took(ref, sem)
        rim_rows[...] = ref[...].astype(jnp.float32).reshape(2 * SIDE, LANES)
        for h in range(2):
            grid[pl.ds(start(f, r, h), SIDE), :] = rim_rows[pl.ds(h, SIDE, stride=2), :]

    pl.when(first)(lambda: rim(rim_lo, rim_sem.at[1], 2, 0))
    pl.when(last)(lambda: rim(rim_hi, rim_sem.at[0], 0, 5))

    took(right0, piece_sem.at[0])
    took(left2, piece_sem.at[1])
    for f, x, ref in ((0, SIDE, right0), (2, -1, left2)):
        for h in range(2):
            grid[pl.ds(start(f, 0, h) + x, 6, stride=2 * PITCH), :] = ref[h].astype(jnp.float32)[:6]

    pl.when(first)(lambda: corners(0))
    pl.when(last)(lambda: corners(5))

    def redo(f, j, h, x, size):
        total = jnp.broadcast_to(weight(dwb_ref, 0, h), (size, LANES))
        turned[pl.ds(slot(f, j, h) + x, size), :] = partial_sum(
            total, f, j, h, x, size, (0, 1, 2))

    def redo_row(f, j):
        for h in range(2):
            for x in (0, 64):
                redo(f, j, h, x, 64)

    pl.when(last)(lambda: redo_row(0, 3))
    pl.when(first)(lambda: redo_row(2, 0))
    for j in range(4):
        for h in range(2):
            redo(0, j, h, SIDE - 8, 8)
            redo(2, j, h, 0, 8)
            if j:
                turned[pl.ds(slot(0, j, h) - j, j), :] = turned[
                    pl.ds(slot(0, j, h) + SIDE - j, j), :]
    pack_1(3, 31)
    recv[1, me] = send[1, me]
    send_family(0)
    pl.when(me != ALL - 1)(
        push(
            send.at[1, ALL - 1], recv.at[1, me], send_sem.at[1], recv_sem.at[1], 3, 31
        ).start)

    c = me
    def coeff(ref, k):
        lo = jnp.broadcast_to(ref[k : k + 1, :LANES], (8, LANES))
        hi = jnp.broadcast_to(ref[k : k + 1, LANES:], (8, LANES))
        odd = lax.rem(lax.broadcasted_iota(jnp.int32, (8, LANES), 0), 2) == 1
        return jnp.where(odd, hi, lo)

    taps = [coeff(zk_ref, k) for k in range(TAPS)]
    bias = coeff(zb_ref, 0)

    def blend(terms):
        products = [tap * term for tap, term in zip(taps, terms)]
        return ((products[0] + products[1]) + (products[2] + products[3])) + (
            (products[4] + products[5]) + (products[6] + bias))

    def arrive(g):
        all_blocks(face, sub, send.at[g], recv.at[g], send_sem.at[g], recv_sem.at[g]).wait_recv()

    def depart(g):
        back_recv[g, me] = back_send[g, me]
        dispatch(
            face, sub, back_send.at[g], back_recv.at[g], send_sem.at[3 + g], recv_sem.at[3 + g])

    block_row = 4 * lax.broadcasted_iota(jnp.int32, (8, 8, LANES), 0) + (
        lax.broadcasted_iota(jnp.int32, (8, 8, LANES), 1) // 2)

    for g in (2, 1):
        arrive(g)

        def unpack(b, carry, g=g):
            at = pl.multiple_of(8 * b, 8)
            i = (3 - (b >> 2)) * 32 + 8 * (b & 3)
            rows = recv[g, pl.ds(i, 8)].astype(jnp.float32)
            if g == 2:
                before = recv[g, pl.ds((i + 96) & (ALL - 1), 8)].astype(jnp.float32)
                rows = jnp.where(block_row + 32 * (b & 3) > c, before, rows)
            chain[pl.ds(at + 3, 8)] = rows
            return carry

        lax.fori_loop(0, 16, unpack, 0, unroll=2)
        for e in range(3):
            chain[e] = chain[ALL + e]
            chain[ALL + 3 + e] = chain[3 + e]

        def stencil_ring(b, carry, g=g):
            at = 8 * b
            i = (3 - (b >> 2)) * 32 + 8 * (b & 3)
            window = [chain[at + n] for n in range(14)]
            for n in range(8):
                total = blend(window[n : n + 7][::-1])
                if g == 1:
                    back_send[g, i + n] = total.astype(jnp.bfloat16)
                else:
                    ring[i + n] = total
            return carry

        lax.fori_loop(0, 16, stencil_ring, 0)
        if g == 2:

            def regroup(b, carry):
                rows = ring[pl.ds(8 * b, 8)]
                after = ring[pl.ds((8 * b + 32) & (ALL - 1), 8)]
                back_send[2, pl.ds(8 * b, 8)] = jnp.where(
                    block_row + 32 * (b & 3) > c, after, rows).astype(jnp.bfloat16)
                return carry

            lax.fori_loop(0, 16, regroup, 0, unroll=2)
        depart(g)

    arrive(0)

    def lay(b, carry):
        rows = recv[0, pl.ds(8 * b, 8)].astype(jnp.float32)
        polar[pl.ds(pl.multiple_of(64 * b, 64), 64), :] = rows.reshape(64, LANES)
        return carry

    lax.fori_loop(0, 16, lay, 0, unroll=2)
    arc_n = SIDE - 1 - c
    arc_s = c + 1
    base_s = BASE_N + 8 * arc_n + 48
    for q in range(4):
        lin[pl.ds(BASE_N + (3 - q) * 2 * arc_n - 2 * (c + 1), 256), :] = polar[
            q * 256 : (q + 1) * 256, :
        ]
    for q in (3, 2, 1, 0):
        lin[pl.ds(base_s + (3 - q) * 2 * arc_s, 256), :] = polar[q * 256 : (q + 1) * 256, :]
    for base, size in ((BASE_N, 8 * arc_n), (base_s, 8 * arc_s)):
        for e in range(3):
            lin[pl.ds(base + size + 8 * e, 8), :] = lin[pl.ds(base + 8 * e, 8), :]
        for e in range(1, 4):
            lin[pl.ds(base - 8 * e, 8), :] = lin[pl.ds(base - 8 * e + size, 8), :]


    def stencil_lin(v, carry):
        at = pl.multiple_of(BASE_N + 64 * v, 8)
        window = [lin[pl.ds(pl.multiple_of(at + 8 * (n - 3), 8), 8), :] for n in range(14)]
        for n in range(8):
            zlin[pl.ds(pl.multiple_of(at + 8 * n, 8), 8), :] = blend(window[n : n + 7][::-1])
        return carry

    lax.fori_loop(0, LIN_BLOCKS, stencil_lin, 0)
    row_256 = lax.broadcasted_iota(jnp.int32, (256, LANES), 0) // 2
    for q in range(4):
        from_n = zlin[pl.ds(BASE_N + (3 - q) * 2 * arc_n - 2 * (c + 1), 256), :]
        from_s = zlin[pl.ds(base_s + (3 - q) * 2 * arc_s, 256), :]
        back_send[0, pl.ds(32 * q, 32)] = (
            jnp.where(row_256 > c, from_n, from_s).reshape(32, 8, LANES).astype(jnp.bfloat16))
    depart(0)

    gain = gain_ref[...]
    scale = ls_ref[...]
    w_in = w_in_ref[...]
    w_out = w_out_ref[...]
    column = lax.broadcasted_iota(jnp.int32, (SIDE, 2 * LANES), 0)

    def mlp(g, j, carry):
        base = g * FACE_ROWS + 2 * j * TURN + j + 8
        values = jnp.concatenate(
            [turned[pl.ds(base, SIDE), :], turned[pl.ds(base + TURN, SIDE), :]], axis=1
        )
        mean = jnp.mean(values, -1, keepdims=True)
        centred = values - mean
        spread = jnp.mean(jnp.square(centred), -1, keepdims=True)
        normed = (centred * lax.rsqrt(spread + 1e-06) * gain).astype(jnp.bfloat16)
        pre = jnp.dot(normed, w_in, preferred_element_type=jnp.float32)
        hidden = (0.5 * pre * (1.0 + lax.erf(pre * np.float32(np.sqrt(0.5))))).astype(jnp.bfloat16)
        branch = jnp.dot(hidden, w_out, preferred_element_type=jnp.float32)
        upper = column + 4 * sub + j >= SIDE
        source = jnp.where(
            upper, field_ref[high[g], j].astype(jnp.float32), field_ref[low[g], j].astype(jnp.float32))
        result = source + scale * branch
        for f, kept in ((high[g], upper), (low[g], jnp.logical_not(upper))):
            seen = (g, f) in ((1, 1), (0, 0), (0, 2))
            row = jnp.where(kept, result, out_ref[f, j].astype(jnp.float32)) if seen else result
            out_ref[f, j] = row.astype(jnp.bfloat16)
        return carry

    for g in (2, 1, 0):
        all_blocks(
            face, sub, back_send.at[g], back_recv.at[g], send_sem.at[3 + g], recv_sem.at[3 + g]
        ).wait_recv()

        def unturn(i, carry, g=g):
            t = (i - 4 * sub) & (ALL - 1)
            turned[pl.ds(g * FACE_ROWS + 8 + t, 8, stride=TURN), :] = back_recv[g, i].astype(
                jnp.float32)
            return carry

        lax.fori_loop(0, ALL, unturn, 0, unroll=8)
        for j in range(1, 4):
            for h in range(2):
                turned[pl.ds(slot(g, j, h) + SIDE - j, j), :] = turned[
                    pl.ds(slot(g, j, h) - j, j), :]
        lax.fori_loop(0, 4, functools.partial(mlp, g), 0)

    for cond, copy in inner:
        pl.when(cond)(copy.wait_send)
    for copy in outer:
        copy.wait_send()
    pl.when(first | last)(
        lambda: push(pieces, pieces, piece_sent, piece_sem.at[0], face, sub).wait_send())
    for g in range(3):
        all_blocks(face, sub, send.at[g], recv.at[g], send_sem.at[g], recv_sem.at[g]).wait_send()
        all_blocks(
            face, sub, back_send.at[g], back_recv.at[g], send_sem.at[3 + g], recv_sem.at[3 + g]
        ).wait_send()


def run(field, dw_kernel, dw_bias, zonal_kernel, zonal_bias, norm_gain, w_in, w_out, layer_scale):
    vmem = pl.BlockSpec(memory_space=pltpu.VMEM)
    lines = pltpu.VMEM((3, SIDE, 2 * LANES), jnp.bfloat16)
    tiles = lambda *lead: pltpu.VMEM((*lead, 8, LANES), jnp.bfloat16)
    rows = lambda n: pltpu.VMEM((n, LANES), jnp.float32)
    vector = pltpu.VMEM((1, 2 * LANES), jnp.float32)
    blocks = pltpu.VMEM((3, ALL, 8, LANES), jnp.bfloat16)
    dma = pltpu.SemaphoreType.DMA
    return pl.pallas_call(
        kernel,
        out_shape=jax.ShapeDtypeStruct(field.shape, jnp.bfloat16),
        in_specs=[pl.BlockSpec(memory_space=pltpu.HBM)] * 9,
        out_specs=vmem,
        scratch_shapes=[
            pltpu.VMEM(field.shape, field.dtype),
            pltpu.VMEM(dw_kernel.shape, jnp.float32),
            vector,
            pltpu.VMEM(zonal_kernel.shape, jnp.float32),
            vector,
            vector,
            pltpu.VMEM(w_in.shape, w_in.dtype),
            pltpu.VMEM(w_out.shape, w_out.dtype),
            vector,
            dma((9,)),
            rows(36 * PITCH + 16),
            lines,
            lines,
            tiles(4),
            tiles(3),
            tiles(3),
            tiles(32, 2),
            tiles(2),
            tiles(2),
            tiles(32),
            tiles(32),
            rows(2 * SIDE),
            rows(3 * FACE_ROWS + 8),
            blocks,
            blocks,
            pltpu.VMEM((ALL + 6, 8, LANES), jnp.float32),
            pltpu.VMEM((ALL, 8, LANES), jnp.float32),
            rows(1024),
            rows(LIN_ROWS),
            rows(LIN_ROWS),
            blocks,
            blocks,
            dma((6,)),
            dma((6,)),
            pltpu.SemaphoreType.REGULAR((2,)),
            dma((2, 3)),
            dma((3,)),
            dma((3,)),
            dma((2, 3)),
            dma((3,)),
            dma((3,)),
            dma,
            dma((2,)),
            dma((2,)),
            dma((2,)),
        ],
        compiler_params=pltpu.CompilerParams(
            collective_id=0, has_side_effects=True, vmem_limit_bytes=24 * 1024 * 1024
        ),
    )(*[pltpu.with_memory_space_constraint(a, pltpu.HBM) for a in (
        field, dw_kernel, dw_bias[None], zonal_kernel, zonal_bias[None], norm_gain[None], w_in,
        w_out, layer_scale[None],
    )])


def shards(
    field, dw_kernel, dw_bias, zonal_kernel, zonal_bias, norm_gain, w_in, w_out, layer_scale
):
    output = run(
        field[:, 0], dw_kernel, dw_bias, zonal_kernel, zonal_bias, norm_gain, w_in, w_out,
        layer_scale,
    )
    return output[:, None]


def solution(mesh):
    in_specs = (P(None, "face", "sub", None, None), P(), P(), P(), P(), P(), P(), P(), P())
    out_specs = P(None, "face", "sub", None, None)
    return jax.shard_map(shards, mesh=mesh, in_specs=in_specs, out_specs=out_specs, check_vma=False)
```

```python
import functools

import jax
import jax.numpy as jnp
import numpy as np
from jax import lax
from jax.experimental import pallas as pl
from jax.experimental.pallas import tpu as pltpu
from jax.sharding import PartitionSpec as P

MESH = pl.DeviceIdType.MESH
TAPS = 7
SIDE = 128
ALL = 128
LANES = 128
PITCH = 137
ROW = 8
TURN = 137
FACE_ROWS = 8 * TURN + 16
BASE_N = 288
LIN_ROWS = 1664
LIN_BLOCKS = 17


def hops(step):
    return sum(min(d, 4 - d) for d in step[:3])


STEPS = sorted(
    (
        (face, x, z, core)
        for face in range(4)
        for x in range(4)
        for z in range(4)
        for core in range(2)
        if face + x + z + core
    ),
    key=lambda step: -hops(step),
)


def peers(face, sub):
    for df, dx, dz, dc in STEPS:
        px = ((sub >> 3) + dx) & 3
        pz = ((sub >> 1) + dz) & 3
        pc = (sub + dc) & 1
        yield (face + df) & 3, (px << 3) + (pz << 1) + pc


def greet(sem, pf, ps):
    pl.semaphore_signal(sem, inc=1, device_id=(pf, ps), device_id_type=MESH)


def announce(face, sub):
    barrier = pltpu.get_barrier_semaphore()
    east = (face + 1) & 3
    west = (face + 3) & 3
    for n in range(1, 8):
        greet(barrier, face, (sub & 24) + ((sub + n) & 7))
    for n in range(1, 4):
        greet(barrier, face, (sub + 8 * n) & 31)
        greet(barrier, (face + n) & 3, sub)
    edge = sub & 7
    for cond, pf, ps in (
        (sub > 0, east, sub - 1),
        (sub > 0, west, sub - 1),
        (sub < 31, east, sub + 1),
        (sub < 31, west, sub + 1),
        ((edge == 7) & (sub < 31), face, sub + 1),
        ((edge == 0) & (sub > 0), face, sub - 1),
        (sub == 31, face, 0),
        (sub == 31, west, 0),
        (sub == 0, face, 31),
        (sub == 0, east, 31),
    ):
        pl.when(cond)(functools.partial(greet, barrier, pf, ps))
    inner_edge = ((edge == 0) | (edge == 7)) & (sub > 0) & (sub < 31)
    return 17 + inner_edge.astype(jnp.int32)


def exchange(face, sub, prepare, source, target, send_sem, recv_sem, later=None):
    me = face * 32 + sub

    def push(pf, ps):
        copy = pltpu.make_async_remote_copy(
            source.at[pf * 32 + ps],
            target.at[me],
            send_sem,
            recv_sem,
            device_id=(pf, ps),
            device_id_type=MESH,
        )
        if later is None:
            copy.start()
        else:
            pl.when(pf * 32 + ps != later)(copy.start)

    waiting = None
    for pf, ps in peers(face, sub):
        prepare(pf, ps)
        if waiting is not None:
            push(*waiting)
        waiting = pf, ps
    push(*waiting)


def dispatch(face, sub, source, target, send_sem, recv_sem):
    me = face * 32 + sub

    for pf, ps in peers(face, sub):
        pltpu.make_async_remote_copy(
            source.at[pf * 32 + ps],
            target.at[me],
            send_sem,
            recv_sem,
            device_id=(pf, ps),
            device_id_type=MESH,
        ).start()


def all_blocks(face, sub, source, target, send_sem, recv_sem):
    return pltpu.make_async_remote_copy(
        source.at[pl.ds(0, ALL - 1)],
        target.at[pl.ds(0, ALL - 1)],
        send_sem,
        recv_sem,
        device_id=(face, sub),
        device_id_type=MESH,
    )


def kernel(
    field_hbm, dwk_hbm, dwb_hbm, zk_hbm, zb_hbm, gain_hbm, w_in_hbm, w_out_hbm, ls_hbm, out_ref,
    field_ref, dwk_ref, dwb_ref, zk_ref, zb_ref, gain_ref, w_in_ref, w_out_ref, ls_ref, load_sem,
    grid, row_lo, row_hi, cols, left1, right2, pieces, right0, left2, rim_hi, rim_lo, rim_rows,
    turned, send, recv, chain, ring, polar, lin, zlin, back_send, back_recv,
    send_sem, recv_sem, round_sem, row_sent, lo_sem, hi_sem, col_sent, left_sem, right_sem, piece_sent,
    piece_sem, rim_sent, rim_sem,
):
    face = lax.axis_index("face")
    sub = lax.axis_index("sub")
    me = face * 32 + sub
    east = (face + 1) & 3
    west = (face + 3) & 3
    first = sub == 0
    last = sub == 31
    loads = [
        pltpu.make_async_copy(source, target, load_sem.at[n])
        for n, (source, target) in enumerate((
            (field_hbm, field_ref), (dwk_hbm, dwk_ref), (dwb_hbm, dwb_ref), (zk_hbm, zk_ref),
            (zb_hbm, zb_ref), (gain_hbm, gain_ref), (w_in_hbm, w_in_ref), (w_out_hbm, w_out_ref),
            (ls_hbm, ls_ref)))
    ]
    loads[0].start()
    partners = announce(face, sub)
    for load in loads[1:]:
        load.start()

    def start(f, r, h=0):
        return (f * 12 + r * 2 + h) * PITCH + ROW

    def push(source, target, sent, got, pf, ps):
        return pltpu.make_async_remote_copy(
            source, target, sent, got, device_id=(pf, ps), device_id_type=MESH
        )

    rows = []
    for f in (2, 1, 0):
        rows.append((sub < 31, push(
            field_hbm.at[f, 3], row_lo.at[f], row_sent.at[0, f], lo_sem.at[f], face, sub + 1)))
        rows.append((sub > 0, push(
            field_hbm.at[f, 0], row_hi.at[f], row_sent.at[1, f], hi_sem.at[f], face, sub - 1)))
        if f:
            rows.append((last, push(
                field_hbm.at[f, 3], row_lo.at[f - 1], row_sent.at[0, f], lo_sem.at[f - 1],
                west if f == 1 else face, 0)))
        if f < 2:
            rows.append((first, push(
                field_hbm.at[f, 0], row_hi.at[f + 1], row_sent.at[1, f], hi_sem.at[f + 1],
                east if f == 0 else face, 31)))
    sides = []
    for d, cond in ((-1, sub > 0), (0, sub >= 0), (1, sub < 31)):
        sides.append((cond, push(
            cols.at[0], left1.at[1 - d], col_sent.at[0, 1 - d], left_sem.at[1 - d], east, sub + d)))
        sides.append((cond, push(
            cols.at[1], right2.at[1 - d], col_sent.at[1, 1 - d], right_sem.at[1 - d], west, sub + d)))
    outer = []
    outer.append(push(
        cols.at[2], rim_hi.at[sub], rim_sent.at[0], rim_sem.at[0], east, 31))
    outer.append(push(
        cols.at[3], rim_lo.at[sub], rim_sent.at[1], rim_sem.at[1], west, 0))

    pl.semaphore_wait(pltpu.get_barrier_semaphore(), partners)
    for cond, copy in rows:
        pl.when(cond)(copy.start)
    for n in range(1, 4):
        greet(round_sem.at[0], face, (sub + 8 * n) & 31)
    loads[0].wait()

    def widen(t, carry):
        f = t >> 2
        j = t & 3
        for h in range(2):
            grid[pl.ds(start(f, j + 1, h), SIDE), :] = field_ref[
                f, j, :, h * LANES : (h + 1) * LANES
            ].astype(jnp.float32)
        return carry

    lax.fori_loop(0, 12, widen, 0)
    for n, (f, x) in enumerate(((2, SIDE - 1), (1, 0), (0, SIDE - 1), (2, 0))):
        cols[n] = grid[pl.ds(start(f, 1) + x, 8, stride=PITCH), :].astype(jnp.bfloat16)

    def cut(base):
        def one(t, carry):
            for h in range(2):
                at = base + h * PITCH + 4 * t - 1
                pieces[t, h] = grid[pl.ds(at, 8), :].astype(jnp.bfloat16)
            return carry

        lax.fori_loop(0, 32, one, 0)

    pl.when(last)(lambda: cut(start(0, 4)))
    pl.when(first)(lambda: cut(start(2, 1)))
    for cond, copy in sides:
        pl.when(cond)(copy.start)
    pl.semaphore_wait(round_sem.at[0], 3)
    for n in range(1, 4):
        greet(round_sem.at[1], (face + n) & 3, sub)
    for load in loads[1:]:
        load.wait()

    def weight(ref, tap, h):
        return ref[tap : tap + 1, h * LANES : (h + 1) * LANES]

    def partial_sum(total, f, j, h, x, size, rows):
        for i in rows:
            for k in range(3):
                at = start(f, j + i, h) + x + k - 1
                total = total + weight(dwk_ref, 3 * i + k, h) * grid[pl.ds(at, size), :]
        return total

    def slot(f, j, h):
        return f * FACE_ROWS + (2 * j + h) * TURN + j + 8

    def inside(f, carry):
        for j in range(4):
            rows = (1, 2) if j == 0 else (0, 1) if j == 3 else (0, 1, 2)
            for h in range(2):
                for x in (8, 64):
                    zero = jnp.broadcast_to(weight(dwb_ref, 0, h), (56, LANES))
                    turned[pl.ds(slot(f, j, h) + x, 56), :] = partial_sum(
                        zero, f, j, h, x, 56, rows)
        return carry

    lax.fori_loop(0, 3, inside, 0)
    pl.semaphore_wait(round_sem.at[1], 3)
    for copy in outer:
        copy.start()

    def scatter(pf, target, got):
        def one(t, carry):
            push(pieces.at[t], target, piece_sent, got, pf, t).start()
            return carry

        lax.fori_loop(0, 32, one, 0)

    pl.when(last)(lambda: scatter(west, right0, piece_sem.at[0]))
    pl.when(first)(lambda: scatter(east, left2, piece_sem.at[1]))

    def took(ref, sem):
        push(ref, ref, row_sent.at[0, 0], sem, face, sub).wait_recv()

    def fill(f):
        pl.when((sub > 0) if f == 2 else (sub >= 0))(lambda: took(row_lo.at[f], lo_sem.at[f]))
        pl.when((sub < 31) if f == 0 else (sub >= 0))(lambda: took(row_hi.at[f], hi_sem.at[f]))
        for h in range(2):
            half = slice(h * LANES, (h + 1) * LANES)
            grid[pl.ds(start(f, 0, h), SIDE), :] = row_lo[f, :, half].astype(jnp.float32)
            grid[pl.ds(start(f, 5, h), SIDE), :] = row_hi[f, :, half].astype(jnp.float32)

    def side(f, x, ref, sem):
        for e, cond in ((0, sub > 0), (1, sub >= 0), (2, sub < 31)):
            pl.when(cond)(lambda e=e: took(ref.at[e], sem.at[e]))
        before = ref[0].astype(jnp.float32)
        after = ref[2].astype(jnp.float32)
        grid[pl.ds(start(f, 0) + x, 2, stride=PITCH), :] = before[6:8]
        grid[pl.ds(start(f, 1) + x, 8, stride=PITCH), :] = ref[1].astype(jnp.float32)
        grid[pl.ds(start(f, 5) + x, 2, stride=PITCH), :] = after[0:2]

    def next_to(f, x, other, at):
        for r, size in ((0, 8), (4, 4)):
            grid[pl.ds(start(f, r) + x, size, stride=PITCH), :] = grid[
                pl.ds(start(other, r) + at, size, stride=PITCH), :]

    def corners(f):
        def clear(r):
            for x in (-1, SIDE):
                grid[pl.ds(start(f, r) + x, 2, stride=PITCH), :] = jnp.zeros(
                    (2, LANES), jnp.float32)

        pl.when(first)(lambda: clear(0))
        pl.when(last)(lambda: clear(5))

    def redo(f, j, h, x, size):
        total = jnp.broadcast_to(weight(dwb_ref, 0, h), (size, LANES))
        turned[pl.ds(slot(f, j, h) + x, size), :] = partial_sum(
            total, f, j, h, x, size, (0, 1, 2))

    def wrap(f):
        for j in range(1, 4):
            for h in range(2):
                turned[pl.ds(slot(f, j, h) - j, j), :] = turned[
                    pl.ds(slot(f, j, h) + SIDE - j, j), :]

    def around(f):
        for j in range(4):
            for h in range(2):
                for x in (0, SIDE - 8):
                    redo(f, j, h, x, 8)
                if j in (0, 3):
                    for x in (8, 64):
                        at = pl.ds(slot(f, j, h) + x, 56)
                        turned[at, :] = partial_sum(
                            turned[at, :], f, j, h, x, 56, (0,) if j == 0 else (2,))
        wrap(f)

    side(2, SIDE, right2, right_sem)
    side(1, -1, left1, left_sem)
    fill(2)
    corners(2)
    around(2)
    fill(1)
    next_to(1, SIDE, 0, 0)
    corners(1)
    around(1)

    high = (0, 1, 2)
    low = (2, 0, 1)
    row_in = lax.broadcasted_iota(jnp.int32, (8, LANES), 0) // 2

    def send_family(g, later=None):
        def pack(pf, ps):
            c = pf * 32 + ps
            t = (c - 4 * sub) & (ALL - 1)
            above = turned[pl.ds(high[g] * FACE_ROWS + 8 + t, 8, stride=TURN), :]
            below = turned[pl.ds(low[g] * FACE_ROWS + 8 + t, 8, stride=TURN), :]
            send[g, c] = jnp.where(row_in + 4 * sub > c, above, below).astype(jnp.bfloat16)

        exchange(
            face, sub, pack, send.at[g], recv.at[g], send_sem.at[g], recv_sem.at[g], later)
        pack(face, sub)
        recv[g, me] = send[g, me]
        return pack

    send_family(2)
    fill(0)
    next_to(0, -1, 1, SIDE - 1)
    next_to(1, SIDE, 0, 0)
    corners(0)
    corners(1)
    around(0)
    for j in (0, 3):
        for h in range(2):
            redo(1, j, h, SIDE - 8, 8)
    wrap(1)
    pack_1 = send_family(1, ALL - 1)

    def rim(ref, sem, f, r):
        took(ref, sem)
        rim_rows[...] = ref[...].astype(jnp.float32).reshape(2 * SIDE, LANES)
        for h in range(2):
            grid[pl.ds(start(f, r, h), SIDE), :] = rim_rows[pl.ds(h, SIDE, stride=2), :]

    pl.when(first)(lambda: rim(rim_lo, rim_sem.at[1], 2, 0))
    pl.when(last)(lambda: rim(rim_hi, rim_sem.at[0], 0, 5))

    took(right0, piece_sem.at[0])
    took(left2, piece_sem.at[1])
    for f, x, ref in ((0, SIDE, right0), (2, -1, left2)):
        for h in range(2):
            grid[pl.ds(start(f, 0, h) + x, 6, stride=2 * PITCH), :] = ref[h].astype(jnp.float32)[:6]

    corners(0)
    corners(2)

    def redo_row(f, j):
        for h in range(2):
            for x in (0, 64):
                redo(f, j, h, x, 64)

    pl.when(last)(lambda: redo_row(0, 3))
    pl.when(first)(lambda: redo_row(2, 0))
    for j in range(4):
        for h in range(2):
            redo(0, j, h, SIDE - 8, 8)
            redo(2, j, h, 0, 8)
    wrap(0)
    pack_1(3, 31)
    recv[1, me] = send[1, me]
    send_family(0)
    pl.when(me != ALL - 1)(
        push(
            send.at[1, ALL - 1], recv.at[1, me], send_sem.at[1], recv_sem.at[1], 3, 31
        ).start)

    c = me
    def coeff(ref, k):
        lo = jnp.broadcast_to(ref[k : k + 1, :LANES], (8, LANES))
        hi = jnp.broadcast_to(ref[k : k + 1, LANES:], (8, LANES))
        odd = lax.rem(lax.broadcasted_iota(jnp.int32, (8, LANES), 0), 2) == 1
        return jnp.where(odd, hi, lo)

    taps = [coeff(zk_ref, k) for k in range(TAPS)]
    bias = coeff(zb_ref, 0)

    def blend(terms):
        products = [tap * term for tap, term in zip(taps, terms)]
        return ((products[0] + products[1]) + (products[2] + products[3])) + (
            (products[4] + products[5]) + (products[6] + bias))

    def arrive(g):
        all_blocks(face, sub, send.at[g], recv.at[g], send_sem.at[g], recv_sem.at[g]).wait_recv()

    def depart(g):
        back_recv[g, me] = back_send[g, me]
        dispatch(
            face, sub, back_send.at[g], back_recv.at[g], send_sem.at[3 + g], recv_sem.at[3 + g])

    block_row = 4 * lax.broadcasted_iota(jnp.int32, (8, 8, LANES), 0) + (
        lax.broadcasted_iota(jnp.int32, (8, 8, LANES), 1) // 2)

    for g in (2, 1):
        arrive(g)

        def unpack(b, carry, g=g):
            at = pl.multiple_of(8 * b, 8)
            i = (3 - (b >> 2)) * 32 + 8 * (b & 3)
            rows = recv[g, pl.ds(i, 8)].astype(jnp.float32)
            if g == 2:
                before = recv[g, pl.ds((i + 96) & (ALL - 1), 8)].astype(jnp.float32)
                rows = jnp.where(block_row + 32 * (b & 3) > c, before, rows)
            chain[pl.ds(at + 3, 8)] = rows
            return carry

        lax.fori_loop(0, 16, unpack, 0, unroll=2)
        for e in range(3):
            chain[e] = chain[ALL + e]
            chain[ALL + 3 + e] = chain[3 + e]

        def stencil_ring(b, carry, g=g):
            at = 8 * b
            i = (3 - (b >> 2)) * 32 + 8 * (b & 3)
            window = [chain[at + n] for n in range(14)]
            for n in range(8):
                total = blend(window[n : n + 7][::-1])
                if g == 1:
                    back_send[g, i + n] = total.astype(jnp.bfloat16)
                else:
                    ring[i + n] = total
            return carry

        lax.fori_loop(0, 16, stencil_ring, 0)
        if g == 2:

            def regroup(b, carry):
                rows = ring[pl.ds(8 * b, 8)]
                after = ring[pl.ds((8 * b + 32) & (ALL - 1), 8)]
                back_send[2, pl.ds(8 * b, 8)] = jnp.where(
                    block_row + 32 * (b & 3) > c, after, rows).astype(jnp.bfloat16)
                return carry

            lax.fori_loop(0, 16, regroup, 0, unroll=2)
        depart(g)

    arrive(0)

    def lay(b, carry):
        rows = recv[0, pl.ds(8 * b, 8)].astype(jnp.float32)
        polar[pl.ds(pl.multiple_of(64 * b, 64), 64), :] = rows.reshape(64, LANES)
        return carry

    lax.fori_loop(0, 16, lay, 0, unroll=2)
    arc_n = SIDE - 1 - c
    arc_s = c + 1
    base_s = BASE_N + 8 * arc_n + 48
    for q in range(4):
        lin[pl.ds(BASE_N + (3 - q) * 2 * arc_n - 2 * (c + 1), 256), :] = polar[
            q * 256 : (q + 1) * 256, :
        ]
    for q in (3, 2, 1, 0):
        lin[pl.ds(base_s + (3 - q) * 2 * arc_s, 256), :] = polar[q * 256 : (q + 1) * 256, :]
    for base, size in ((BASE_N, 8 * arc_n), (base_s, 8 * arc_s)):
        for e in range(3):
            lin[pl.ds(base + size + 8 * e, 8), :] = lin[pl.ds(base + 8 * e, 8), :]
        for e in range(1, 4):
            lin[pl.ds(base - 8 * e, 8), :] = lin[pl.ds(base - 8 * e + size, 8), :]


    def stencil_lin(v, carry):
        at = pl.multiple_of(BASE_N + 64 * v, 8)
        window = [lin[pl.ds(pl.multiple_of(at + 8 * (n - 3), 8), 8), :] for n in range(14)]
        for n in range(8):
            zlin[pl.ds(pl.multiple_of(at + 8 * n, 8), 8), :] = blend(window[n : n + 7][::-1])
        return carry

    lax.fori_loop(0, LIN_BLOCKS, stencil_lin, 0)
    row_256 = lax.broadcasted_iota(jnp.int32, (256, LANES), 0) // 2
    for q in range(4):
        from_n = zlin[pl.ds(BASE_N + (3 - q) * 2 * arc_n - 2 * (c + 1), 256), :]
        from_s = zlin[pl.ds(base_s + (3 - q) * 2 * arc_s, 256), :]
        back_send[0, pl.ds(32 * q, 32)] = (
            jnp.where(row_256 > c, from_n, from_s).reshape(32, 8, LANES).astype(jnp.bfloat16))
    depart(0)

    gain = gain_ref[...]
    scale = ls_ref[...]
    w_in = w_in_ref[...]
    w_out = w_out_ref[...]
    column = lax.broadcasted_iota(jnp.int32, (SIDE, 2 * LANES), 0)

    def mlp(g, j, carry):
        base = g * FACE_ROWS + 2 * j * TURN + j + 8
        values = jnp.concatenate(
            [turned[pl.ds(base, SIDE), :], turned[pl.ds(base + TURN, SIDE), :]], axis=1
        )
        mean = jnp.mean(values, -1, keepdims=True)
        centred = values - mean
        spread = jnp.mean(jnp.square(centred), -1, keepdims=True)
        normed = (centred * lax.rsqrt(spread + 1e-06) * gain).astype(jnp.bfloat16)
        pre = jnp.dot(normed, w_in, preferred_element_type=jnp.float32)
        hidden = (0.5 * pre * (1.0 + lax.erf(pre * np.float32(np.sqrt(0.5))))).astype(jnp.bfloat16)
        branch = jnp.dot(hidden, w_out, preferred_element_type=jnp.float32)
        upper = column + 4 * sub + j >= SIDE
        source = jnp.where(
            upper, field_ref[high[g], j].astype(jnp.float32), field_ref[low[g], j].astype(jnp.float32))
        result = source + scale * branch
        for f, kept in ((high[g], upper), (low[g], jnp.logical_not(upper))):
            seen = (g, f) in ((1, 1), (0, 0), (0, 2))
            row = jnp.where(kept, result, out_ref[f, j].astype(jnp.float32)) if seen else result
            out_ref[f, j] = row.astype(jnp.bfloat16)
        return carry

    for g in (2, 1, 0):
        all_blocks(
            face, sub, back_send.at[g], back_recv.at[g], send_sem.at[3 + g], recv_sem.at[3 + g]
        ).wait_recv()

        def unturn(i, carry, g=g):
            t = (i - 4 * sub) & (ALL - 1)
            turned[pl.ds(g * FACE_ROWS + 8 + t, 8, stride=TURN), :] = back_recv[g, i].astype(
                jnp.float32)
            return carry

        lax.fori_loop(0, ALL, unturn, 0, unroll=8)
        for j in range(1, 4):
            for h in range(2):
                turned[pl.ds(slot(g, j, h) + SIDE - j, j), :] = turned[
                    pl.ds(slot(g, j, h) - j, j), :]
        lax.fori_loop(0, 4, functools.partial(mlp, g), 0, unroll=4)

    for cond, copy in rows + sides:
        pl.when(cond)(copy.wait_send)
    for copy in outer:
        copy.wait_send()
    pl.when(first | last)(
        lambda: push(pieces, pieces, piece_sent, piece_sem.at[0], face, sub).wait_send())
    for g in range(3):
        all_blocks(face, sub, send.at[g], recv.at[g], send_sem.at[g], recv_sem.at[g]).wait_send()
        all_blocks(
            face, sub, back_send.at[g], back_recv.at[g], send_sem.at[3 + g], recv_sem.at[3 + g]
        ).wait_send()


def run(field, dw_kernel, dw_bias, zonal_kernel, zonal_bias, norm_gain, w_in, w_out, layer_scale):
    vmem = pl.BlockSpec(memory_space=pltpu.VMEM)
    lines = pltpu.VMEM((3, SIDE, 2 * LANES), jnp.bfloat16)
    tiles = lambda *lead: pltpu.VMEM((*lead, 8, LANES), jnp.bfloat16)
    rows = lambda n: pltpu.VMEM((n, LANES), jnp.float32)
    vector = pltpu.VMEM((1, 2 * LANES), jnp.float32)
    blocks = pltpu.VMEM((3, ALL, 8, LANES), jnp.bfloat16)
    dma = pltpu.SemaphoreType.DMA
    return pl.pallas_call(
        kernel,
        out_shape=jax.ShapeDtypeStruct(field.shape, jnp.bfloat16),
        in_specs=[pl.BlockSpec(memory_space=pltpu.HBM)] * 9,
        out_specs=vmem,
        scratch_shapes=[
            pltpu.VMEM(field.shape, field.dtype),
            pltpu.VMEM(dw_kernel.shape, jnp.float32),
            vector,
            pltpu.VMEM(zonal_kernel.shape, jnp.float32),
            vector,
            vector,
            pltpu.VMEM(w_in.shape, w_in.dtype),
            pltpu.VMEM(w_out.shape, w_out.dtype),
            vector,
            dma((9,)),
            rows(36 * PITCH + 16),
            lines,
            lines,
            tiles(4),
            tiles(3),
            tiles(3),
            tiles(32, 2),
            tiles(2),
            tiles(2),
            tiles(32),
            tiles(32),
            rows(2 * SIDE),
            rows(3 * FACE_ROWS + 8),
            blocks,
            blocks,
            pltpu.VMEM((ALL + 6, 8, LANES), jnp.float32),
            pltpu.VMEM((ALL, 8, LANES), jnp.float32),
            rows(1024),
            rows(LIN_ROWS),
            rows(LIN_ROWS),
            blocks,
            blocks,
            dma((6,)),
            dma((6,)),
            pltpu.SemaphoreType.REGULAR((2,)),
            dma((2, 3)),
            dma((3,)),
            dma((3,)),
            dma((2, 3)),
            dma((3,)),
            dma((3,)),
            dma,
            dma((2,)),
            dma((2,)),
            dma((2,)),
        ],
        compiler_params=pltpu.CompilerParams(
            collective_id=0, has_side_effects=True, vmem_limit_bytes=24 * 1024 * 1024
        ),
    )(*[pltpu.with_memory_space_constraint(a, pltpu.HBM) for a in (
        field, dw_kernel, dw_bias[None], zonal_kernel, zonal_bias[None], norm_gain[None], w_in,
        w_out, layer_scale[None],
    )])


def shards(
    field, dw_kernel, dw_bias, zonal_kernel, zonal_bias, norm_gain, w_in, w_out, layer_scale
):
    output = run(
        field[:, 0], dw_kernel, dw_bias, zonal_kernel, zonal_bias, norm_gain, w_in, w_out,
        layer_scale,
    )
    return output[:, None]


def solution(mesh):
    in_specs = (P(None, "face", "sub", None, None), P(), P(), P(), P(), P(), P(), P(), P())
    out_specs = P(None, "face", "sub", None, None)
    return jax.shard_map(shards, mesh=mesh, in_specs=in_specs, out_specs=out_specs, check_vma=False)
```

```python
import functools

import jax
import jax.numpy as jnp
import numpy as np
from jax import lax
from jax.experimental import pallas as pl
from jax.experimental.pallas import tpu as pltpu
from jax.sharding import PartitionSpec as P

MESH = pl.DeviceIdType.MESH
TAPS = 7
SIDE = 128
ALL = 128
LANES = 128
PITCH = 137
ROW = 8
TURN = 137
FACE_ROWS = 8 * TURN + 16
BASE_N = 288
LIN_ROWS = 1664
LIN_BLOCKS = 17


def hops(step):
    return sum(min(d, 4 - d) for d in step[:3])


STEPS = sorted(
    (
        (face, x, z, core)
        for face in range(4)
        for x in range(4)
        for z in range(4)
        for core in range(2)
        if face + x + z + core
    ),
    key=lambda step: -hops(step),
)


def peers(face, sub):
    for df, dx, dz, dc in STEPS:
        px = ((sub >> 3) + dx) & 3
        pz = ((sub >> 1) + dz) & 3
        pc = (sub + dc) & 1
        yield (face + df) & 3, (px << 3) + (pz << 1) + pc


def greet(sem, pf, ps):
    pl.semaphore_signal(sem, inc=1, device_id=(pf, ps), device_id_type=MESH)


def announce(face, sub):
    barrier = pltpu.get_barrier_semaphore()
    east = (face + 1) & 3
    west = (face + 3) & 3
    for n in range(1, 8):
        greet(barrier, face, (sub & 24) + ((sub + n) & 7))
    for n in range(1, 4):
        greet(barrier, face, (sub + 8 * n) & 31)
        greet(barrier, (face + n) & 3, sub)
    edge = sub & 7
    for cond, pf, ps in (
        (sub > 0, east, sub - 1),
        (sub > 0, west, sub - 1),
        (sub < 31, east, sub + 1),
        (sub < 31, west, sub + 1),
        ((edge == 7) & (sub < 31), face, sub + 1),
        ((edge == 0) & (sub > 0), face, sub - 1),
        (sub == 31, face, 0),
        (sub == 31, west, 0),
        (sub == 0, face, 31),
        (sub == 0, east, 31),
    ):
        pl.when(cond)(functools.partial(greet, barrier, pf, ps))
    inner_edge = ((edge == 0) | (edge == 7)) & (sub > 0) & (sub < 31)
    return 17 + inner_edge.astype(jnp.int32)


def exchange(face, sub, prepare, source, target, send_sem, recv_sem, ready=None):
    me = face * 32 + sub

    def push(pf, ps):
        copy = pltpu.make_async_remote_copy(
            source.at[pf * 32 + ps],
            target.at[me],
            send_sem,
            recv_sem,
            device_id=(pf, ps),
            device_id_type=MESH,
        )
        if ready is None:
            copy.start()
        else:
            pl.when(ready(pf * 32 + ps))(copy.start)

    waiting = None
    for pf, ps in peers(face, sub):
        prepare(pf, ps)
        if waiting is not None:
            push(*waiting)
        waiting = pf, ps
    push(*waiting)


def dispatch(face, sub, source, target, send_sem, recv_sem):
    me = face * 32 + sub

    for pf, ps in peers(face, sub):
        pltpu.make_async_remote_copy(
            source.at[pf * 32 + ps],
            target.at[me],
            send_sem,
            recv_sem,
            device_id=(pf, ps),
            device_id_type=MESH,
        ).start()


def all_blocks(face, sub, source, target, send_sem, recv_sem):
    return pltpu.make_async_remote_copy(
        source.at[pl.ds(0, ALL - 1)],
        target.at[pl.ds(0, ALL - 1)],
        send_sem,
        recv_sem,
        device_id=(face, sub),
        device_id_type=MESH,
    )


def kernel(
    field_hbm, dwk_hbm, dwb_hbm, zk_hbm, zb_hbm, gain_hbm, w_in_hbm, w_out_hbm, ls_hbm, out_ref,
    field_ref, dwk_ref, dwb_ref, zk_ref, zb_ref, gain_ref, w_in_ref, w_out_ref, ls_ref, load_sem,
    grid, row_lo, row_hi, cols, left1, right2, pieces, right0, left2, rim_hi, rim_lo, rim_rows,
    turned, send, recv, chain, ring, polar, lin, zlin, back_send, back_recv,
    send_sem, recv_sem, round_sem, row_sent, lo_sem, hi_sem, col_sent, left_sem, right_sem, piece_sent,
    piece_sem, rim_sent, rim_sem,
):
    face = lax.axis_index("face")
    sub = lax.axis_index("sub")
    me = face * 32 + sub
    east = (face + 1) & 3
    west = (face + 3) & 3
    first = sub == 0
    last = sub == 31
    loads = [
        pltpu.make_async_copy(source, target, load_sem.at[n])
        for n, (source, target) in enumerate((
            (field_hbm, field_ref), (dwk_hbm, dwk_ref), (dwb_hbm, dwb_ref), (zk_hbm, zk_ref),
            (zb_hbm, zb_ref), (gain_hbm, gain_ref), (w_in_hbm, w_in_ref), (w_out_hbm, w_out_ref),
            (ls_hbm, ls_ref)))
    ]
    loads[0].start()
    partners = announce(face, sub)
    for load in loads[1:]:
        load.start()

    def start(f, r, h=0):
        return (f * 12 + r * 2 + h) * PITCH + ROW

    def push(source, target, sent, got, pf, ps):
        return pltpu.make_async_remote_copy(
            source, target, sent, got, device_id=(pf, ps), device_id_type=MESH
        )

    rows = []
    for f in (2, 1, 0):
        rows.append((sub < 31, push(
            field_hbm.at[f, 3], row_lo.at[f], row_sent.at[0, f], lo_sem.at[f], face, sub + 1)))
        rows.append((sub > 0, push(
            field_hbm.at[f, 0], row_hi.at[f], row_sent.at[1, f], hi_sem.at[f], face, sub - 1)))
        if f:
            rows.append((last, push(
                field_hbm.at[f, 3], row_lo.at[f - 1], row_sent.at[0, f], lo_sem.at[f - 1],
                west if f == 1 else face, 0)))
        if f < 2:
            rows.append((first, push(
                field_hbm.at[f, 0], row_hi.at[f + 1], row_sent.at[1, f], hi_sem.at[f + 1],
                east if f == 0 else face, 31)))
    sides = []
    for d, cond in ((-1, sub > 0), (0, sub >= 0), (1, sub < 31)):
        sides.append((cond, push(
            cols.at[0], left1.at[1 - d], col_sent.at[0, 1 - d], left_sem.at[1 - d], east, sub + d)))
        sides.append((cond, push(
            cols.at[1], right2.at[1 - d], col_sent.at[1, 1 - d], right_sem.at[1 - d], west, sub + d)))
    outer = []
    outer.append(push(
        cols.at[2], rim_hi.at[sub], rim_sent.at[0], rim_sem.at[0], east, 31))
    outer.append(push(
        cols.at[3], rim_lo.at[sub], rim_sent.at[1], rim_sem.at[1], west, 0))

    pl.semaphore_wait(pltpu.get_barrier_semaphore(), partners)
    for n in range(1, 4):
        greet(round_sem.at[0], face, (sub + 8 * n) & 31)
    for cond, copy in rows:
        pl.when(cond)(copy.start)
    loads[0].wait()

    def widen(t, carry):
        f = t >> 2
        j = t & 3
        for h in range(2):
            grid[pl.ds(start(f, j + 1, h), SIDE), :] = field_ref[
                f, j, :, h * LANES : (h + 1) * LANES
            ].astype(jnp.float32)
        return carry

    for f, x in ((2, SIDE - 16), (1, 0)):
        for j in range(4):
            for h in range(2):
                grid[pl.ds(start(f, j + 1, h) + x, 16), :] = field_ref[
                    f, j, x : x + 16, h * LANES : (h + 1) * LANES
                ].astype(jnp.float32)

    def column(n, f, x):
        cols[n] = grid[pl.ds(start(f, 1) + x, 8, stride=PITCH), :].astype(jnp.bfloat16)

    column(0, 2, SIDE - 1)
    column(1, 1, 0)
    lax.fori_loop(0, 6, widen, 0)
    for cond, copy in sides:
        pl.when(cond)(copy.start)
    lax.fori_loop(6, 12, widen, 0)
    column(2, 0, SIDE - 1)
    column(3, 2, 0)

    def cut(base):
        def one(t, carry):
            for h in range(2):
                at = base + h * PITCH + 4 * t - 1
                pieces[t, h] = grid[pl.ds(at, 8), :].astype(jnp.bfloat16)
            return carry

        lax.fori_loop(0, 32, one, 0)

    pl.when(last)(lambda: cut(start(0, 4)))
    pl.when(first)(lambda: cut(start(2, 1)))
    for load in loads[1:]:
        load.wait()

    def weight(ref, tap, h):
        return ref[tap : tap + 1, h * LANES : (h + 1) * LANES]

    def partial_sum(total, f, j, h, x, size, rows):
        for i in rows:
            for k in range(3):
                at = start(f, j + i, h) + x + k - 1
                total = total + weight(dwk_ref, 3 * i + k, h) * grid[pl.ds(at, size), :]
        return total

    def slot(f, j, h):
        return f * FACE_ROWS + (2 * j + h) * TURN + j + 8

    def inside(f, carry):
        for j in range(4):
            rows = (1, 2) if j == 0 else (0, 1) if j == 3 else (0, 1, 2)
            for h in range(2):
                for x in (8, 64):
                    zero = jnp.broadcast_to(weight(dwb_ref, 0, h), (56, LANES))
                    turned[pl.ds(slot(f, j, h) + x, 56), :] = partial_sum(
                        zero, f, j, h, x, 56, rows)
        return carry

    inside(2, 0)
    pl.semaphore_wait(round_sem.at[0], 3)
    for n in range(1, 4):
        greet(round_sem.at[1], (face + n) & 3, sub)
    lax.fori_loop(0, 2, inside, 0)
    pl.semaphore_wait(round_sem.at[1], 3)
    for copy in outer:
        copy.start()

    def scatter(pf, target, got):
        def one(t, carry):
            push(pieces.at[t], target, piece_sent, got, pf, t).start()
            return carry

        lax.fori_loop(0, 32, one, 0)

    pl.when(last)(lambda: scatter(west, right0, piece_sem.at[0]))
    pl.when(first)(lambda: scatter(east, left2, piece_sem.at[1]))

    def took(ref, sem):
        push(ref, ref, row_sent.at[0, 0], sem, face, sub).wait_recv()

    def fill(f):
        pl.when((sub > 0) if f == 2 else (sub >= 0))(lambda: took(row_lo.at[f], lo_sem.at[f]))
        pl.when((sub < 31) if f == 0 else (sub >= 0))(lambda: took(row_hi.at[f], hi_sem.at[f]))
        for h in range(2):
            half = slice(h * LANES, (h + 1) * LANES)
            grid[pl.ds(start(f, 0, h), SIDE), :] = row_lo[f, :, half].astype(jnp.float32)
            grid[pl.ds(start(f, 5, h), SIDE), :] = row_hi[f, :, half].astype(jnp.float32)

    def side(f, x, ref, sem):
        for e, cond in ((0, sub > 0), (1, sub >= 0), (2, sub < 31)):
            pl.when(cond)(lambda e=e: took(ref.at[e], sem.at[e]))
        before = ref[0].astype(jnp.float32)
        after = ref[2].astype(jnp.float32)
        grid[pl.ds(start(f, 0) + x, 2, stride=PITCH), :] = before[6:8]
        grid[pl.ds(start(f, 1) + x, 8, stride=PITCH), :] = ref[1].astype(jnp.float32)
        grid[pl.ds(start(f, 5) + x, 2, stride=PITCH), :] = after[0:2]

    def next_to(f, x, other, at):
        for r, size in ((0, 8), (4, 4)):
            grid[pl.ds(start(f, r) + x, size, stride=PITCH), :] = grid[
                pl.ds(start(other, r) + at, size, stride=PITCH), :]

    def corners(f):
        def clear(r):
            for x in (-1, SIDE):
                grid[pl.ds(start(f, r) + x, 2, stride=PITCH), :] = jnp.zeros(
                    (2, LANES), jnp.float32)

        pl.when(first)(lambda: clear(0))
        pl.when(last)(lambda: clear(5))

    def redo(f, j, h, x, size):
        total = jnp.broadcast_to(weight(dwb_ref, 0, h), (size, LANES))
        turned[pl.ds(slot(f, j, h) + x, size), :] = partial_sum(
            total, f, j, h, x, size, (0, 1, 2))

    def wrap(f):
        for j in range(1, 4):
            for h in range(2):
                turned[pl.ds(slot(f, j, h) - j, j), :] = turned[
                    pl.ds(slot(f, j, h) + SIDE - j, j), :]

    def around(f):
        for j in range(4):
            for h in range(2):
                for x in (0, SIDE - 8):
                    redo(f, j, h, x, 8)
                if j in (0, 3):
                    for x in (8, 64):
                        at = pl.ds(slot(f, j, h) + x, 56)
                        turned[at, :] = partial_sum(
                            turned[at, :], f, j, h, x, 56, (0,) if j == 0 else (2,))
        wrap(f)

    side(2, SIDE, right2, right_sem)
    side(1, -1, left1, left_sem)
    fill(2)
    corners(2)
    around(2)
    fill(1)
    next_to(1, SIDE, 0, 0)
    corners(1)
    around(1)

    high = (0, 1, 2)
    low = (2, 0, 1)
    row_in = lax.broadcasted_iota(jnp.int32, (8, LANES), 0) // 2

    def send_family(g, ready=None):
        def pack(pf, ps):
            c = pf * 32 + ps
            t = (c - 4 * sub) & (ALL - 1)
            above = turned[pl.ds(high[g] * FACE_ROWS + 8 + t, 8, stride=TURN), :]
            below = turned[pl.ds(low[g] * FACE_ROWS + 8 + t, 8, stride=TURN), :]
            send[g, c] = jnp.where(row_in + 4 * sub > c, above, below).astype(jnp.bfloat16)

        exchange(
            face, sub, pack, send.at[g], recv.at[g], send_sem.at[g], recv_sem.at[g], ready)
        pack(face, sub)
        recv[g, me] = send[g, me]
        return pack

    send_family(2)
    fill(0)
    next_to(0, -1, 1, SIDE - 1)
    next_to(1, SIDE, 0, 0)
    corners(0)
    corners(1)
    around(0)
    for j in (0, 3):
        for h in range(2):
            redo(1, j, h, SIDE - 8, 8)
    wrap(1)
    rim_device = first | last
    pack_1 = send_family(1, lambda owner: (owner != ALL - 1) | ~rim_device)

    def rim(ref, sem, f, r):
        took(ref, sem)
        rim_rows[...] = ref[...].astype(jnp.float32).reshape(2 * SIDE, LANES)
        for h in range(2):
            grid[pl.ds(start(f, r, h), SIDE), :] = rim_rows[pl.ds(h, SIDE, stride=2), :]

    pl.when(first)(lambda: rim(rim_lo, rim_sem.at[1], 2, 0))
    pl.when(last)(lambda: rim(rim_hi, rim_sem.at[0], 0, 5))

    took(right0, piece_sem.at[0])
    took(left2, piece_sem.at[1])
    for f, x, ref in ((0, SIDE, right0), (2, -1, left2)):
        for h in range(2):
            grid[pl.ds(start(f, 0, h) + x, 6, stride=2 * PITCH), :] = ref[h].astype(jnp.float32)[:6]

    corners(0)
    corners(2)

    def redo_row(f, j):
        for h in range(2):
            for x in (0, 64):
                redo(f, j, h, x, 64)

    pl.when(last)(lambda: redo_row(0, 3))
    pl.when(first)(lambda: redo_row(2, 0))
    for j in range(4):
        for h in range(2):
            redo(0, j, h, SIDE - 8, 8)
    wrap(0)

    def pack_last():
        pack_1(3, 31)
        recv[1, me] = send[1, me]

    pl.when(rim_device)(pack_last)
    for j in range(4):
        for h in range(2):
            redo(2, j, h, 0, 8)
    pl.when(rim_device & (me != ALL - 1))(
        push(
            send.at[1, ALL - 1], recv.at[1, me], send_sem.at[1], recv_sem.at[1], 3, 31
        ).start)
    send_family(0)

    c = me
    def coeff(ref, k):
        lo = jnp.broadcast_to(ref[k : k + 1, :LANES], (8, LANES))
        hi = jnp.broadcast_to(ref[k : k + 1, LANES:], (8, LANES))
        odd = lax.rem(lax.broadcasted_iota(jnp.int32, (8, LANES), 0), 2) == 1
        return jnp.where(odd, hi, lo)

    taps = [coeff(zk_ref, k) for k in range(TAPS)]
    bias = coeff(zb_ref, 0)

    def blend(terms):
        products = [tap * term for tap, term in zip(taps, terms)]
        return ((products[0] + products[1]) + (products[2] + products[3])) + (
            (products[4] + products[5]) + (products[6] + bias))

    def arrive(g):
        all_blocks(face, sub, send.at[g], recv.at[g], send_sem.at[g], recv_sem.at[g]).wait_recv()

    def depart(g):
        back_recv[g, me] = back_send[g, me]
        dispatch(
            face, sub, back_send.at[g], back_recv.at[g], send_sem.at[3 + g], recv_sem.at[3 + g])

    block_row = 4 * lax.broadcasted_iota(jnp.int32, (8, 8, LANES), 0) + (
        lax.broadcasted_iota(jnp.int32, (8, 8, LANES), 1) // 2)

    for g in (2, 1):
        arrive(g)

        def unpack(b, carry, g=g):
            at = pl.multiple_of(8 * b, 8)
            i = (3 - (b >> 2)) * 32 + 8 * (b & 3)
            rows = recv[g, pl.ds(i, 8)].astype(jnp.float32)
            if g == 2:
                before = recv[g, pl.ds((i + 96) & (ALL - 1), 8)].astype(jnp.float32)
                rows = jnp.where(block_row + 32 * (b & 3) > c, before, rows)
            chain[pl.ds(at + 3, 8)] = rows
            return carry

        lax.fori_loop(0, 16, unpack, 0, unroll=2)
        for e in range(3):
            chain[e] = chain[ALL + e]
            chain[ALL + 3 + e] = chain[3 + e]

        def stencil_ring(b, carry, g=g):
            at = 8 * b
            i = (3 - (b >> 2)) * 32 + 8 * (b & 3)
            window = [chain[at + n] for n in range(14)]
            for n in range(8):
                total = blend(window[n : n + 7][::-1])
                if g == 1:
                    back_send[g, i + n] = total.astype(jnp.bfloat16)
                else:
                    ring[i + n] = total
            return carry

        lax.fori_loop(0, 16, stencil_ring, 0)
        if g == 2:

            def regroup(b, carry):
                rows = ring[pl.ds(8 * b, 8)]
                after = ring[pl.ds((8 * b + 32) & (ALL - 1), 8)]
                back_send[2, pl.ds(8 * b, 8)] = jnp.where(
                    block_row + 32 * (b & 3) > c, after, rows).astype(jnp.bfloat16)
                return carry

            lax.fori_loop(0, 16, regroup, 0, unroll=2)
        depart(g)

    arrive(0)

    def lay(b, carry):
        rows = recv[0, pl.ds(8 * b, 8)].astype(jnp.float32)
        polar[pl.ds(pl.multiple_of(64 * b, 64), 64), :] = rows.reshape(64, LANES)
        return carry

    lax.fori_loop(0, 16, lay, 0, unroll=2)
    arc_n = SIDE - 1 - c
    arc_s = c + 1
    base_s = BASE_N + 8 * arc_n + 48
    for q in range(4):
        lin[pl.ds(BASE_N + (3 - q) * 2 * arc_n - 2 * (c + 1), 256), :] = polar[
            q * 256 : (q + 1) * 256, :
        ]
    for q in (3, 2, 1, 0):
        lin[pl.ds(base_s + (3 - q) * 2 * arc_s, 256), :] = polar[q * 256 : (q + 1) * 256, :]
    for base, size in ((BASE_N, 8 * arc_n), (base_s, 8 * arc_s)):
        for e in range(3):
            lin[pl.ds(base + size + 8 * e, 8), :] = lin[pl.ds(base + 8 * e, 8), :]
        for e in range(1, 4):
            lin[pl.ds(base - 8 * e, 8), :] = lin[pl.ds(base - 8 * e + size, 8), :]


    def stencil_lin(v, carry):
        at = pl.multiple_of(BASE_N + 64 * v, 8)
        window = [lin[pl.ds(pl.multiple_of(at + 8 * (n - 3), 8), 8), :] for n in range(14)]
        for n in range(8):
            zlin[pl.ds(pl.multiple_of(at + 8 * n, 8), 8), :] = blend(window[n : n + 7][::-1])
        return carry

    lax.fori_loop(0, LIN_BLOCKS, stencil_lin, 0)
    row_256 = lax.broadcasted_iota(jnp.int32, (256, LANES), 0) // 2
    for q in range(4):
        from_n = zlin[pl.ds(BASE_N + (3 - q) * 2 * arc_n - 2 * (c + 1), 256), :]
        from_s = zlin[pl.ds(base_s + (3 - q) * 2 * arc_s, 256), :]
        back_send[0, pl.ds(32 * q, 32)] = (
            jnp.where(row_256 > c, from_n, from_s).reshape(32, 8, LANES).astype(jnp.bfloat16))
    depart(0)

    gain = gain_ref[...]
    scale = ls_ref[...]
    w_in = w_in_ref[...]
    w_out = w_out_ref[...]
    column = lax.broadcasted_iota(jnp.int32, (SIDE, 2 * LANES), 0)

    def mlp(g, j, carry):
        base = g * FACE_ROWS + 2 * j * TURN + j + 8
        values = jnp.concatenate(
            [turned[pl.ds(base, SIDE), :], turned[pl.ds(base + TURN, SIDE), :]], axis=1
        )
        mean = jnp.mean(values, -1, keepdims=True)
        centred = values - mean
        spread = jnp.mean(jnp.square(centred), -1, keepdims=True)
        normed = (centred * lax.rsqrt(spread + 1e-06) * gain).astype(jnp.bfloat16)
        pre = jnp.dot(normed, w_in, preferred_element_type=jnp.float32)
        hidden = (0.5 * pre * (1.0 + lax.erf(pre * np.float32(np.sqrt(0.5))))).astype(jnp.bfloat16)
        branch = jnp.dot(hidden, w_out, preferred_element_type=jnp.float32)
        upper = column + 4 * sub + j >= SIDE
        source = jnp.where(
            upper, field_ref[high[g], j].astype(jnp.float32), field_ref[low[g], j].astype(jnp.float32))
        result = source + scale * branch
        for f, kept in ((high[g], upper), (low[g], jnp.logical_not(upper))):
            seen = (g, f) in ((1, 1), (0, 0), (0, 2))
            row = jnp.where(kept, result, out_ref[f, j].astype(jnp.float32)) if seen else result
            out_ref[f, j] = row.astype(jnp.bfloat16)
        return carry

    for g in (2, 1, 0):
        all_blocks(
            face, sub, back_send.at[g], back_recv.at[g], send_sem.at[3 + g], recv_sem.at[3 + g]
        ).wait_recv()

        def unturn(i, carry, g=g):
            t = (i - 4 * sub) & (ALL - 1)
            turned[pl.ds(g * FACE_ROWS + 8 + t, 8, stride=TURN), :] = back_recv[g, i].astype(
                jnp.float32)
            return carry

        lax.fori_loop(0, ALL, unturn, 0, unroll=8)
        for j in range(1, 4):
            for h in range(2):
                turned[pl.ds(slot(g, j, h) + SIDE - j, j), :] = turned[
                    pl.ds(slot(g, j, h) - j, j), :]
        lax.fori_loop(0, 4, functools.partial(mlp, g), 0, unroll=4)

    for cond, copy in rows + sides:
        pl.when(cond)(copy.wait_send)
    for copy in outer:
        copy.wait_send()
    pl.when(first | last)(
        lambda: push(pieces, pieces, piece_sent, piece_sem.at[0], face, sub).wait_send())
    for g in range(3):
        all_blocks(face, sub, send.at[g], recv.at[g], send_sem.at[g], recv_sem.at[g]).wait_send()
        all_blocks(
            face, sub, back_send.at[g], back_recv.at[g], send_sem.at[3 + g], recv_sem.at[3 + g]
        ).wait_send()


def run(field, dw_kernel, dw_bias, zonal_kernel, zonal_bias, norm_gain, w_in, w_out, layer_scale):
    vmem = pl.BlockSpec(memory_space=pltpu.VMEM)
    lines = pltpu.VMEM((3, SIDE, 2 * LANES), jnp.bfloat16)
    tiles = lambda *lead: pltpu.VMEM((*lead, 8, LANES), jnp.bfloat16)
    rows = lambda n: pltpu.VMEM((n, LANES), jnp.float32)
    vector = pltpu.VMEM((1, 2 * LANES), jnp.float32)
    blocks = pltpu.VMEM((3, ALL, 8, LANES), jnp.bfloat16)
    dma = pltpu.SemaphoreType.DMA
    return pl.pallas_call(
        kernel,
        out_shape=jax.ShapeDtypeStruct(field.shape, jnp.bfloat16),
        in_specs=[pl.BlockSpec(memory_space=pltpu.HBM)] * 9,
        out_specs=vmem,
        scratch_shapes=[
            pltpu.VMEM(field.shape, field.dtype),
            pltpu.VMEM(dw_kernel.shape, jnp.float32),
            vector,
            pltpu.VMEM(zonal_kernel.shape, jnp.float32),
            vector,
            vector,
            pltpu.VMEM(w_in.shape, w_in.dtype),
            pltpu.VMEM(w_out.shape, w_out.dtype),
            vector,
            dma((9,)),
            rows(36 * PITCH + 16),
            lines,
            lines,
            tiles(4),
            tiles(3),
            tiles(3),
            tiles(32, 2),
            tiles(2),
            tiles(2),
            tiles(32),
            tiles(32),
            rows(2 * SIDE),
            rows(3 * FACE_ROWS + 8),
            blocks,
            blocks,
            pltpu.VMEM((ALL + 6, 8, LANES), jnp.float32),
            pltpu.VMEM((ALL, 8, LANES), jnp.float32),
            rows(1024),
            rows(LIN_ROWS),
            rows(LIN_ROWS),
            blocks,
            blocks,
            dma((6,)),
            dma((6,)),
            pltpu.SemaphoreType.REGULAR((2,)),
            dma((2, 3)),
            dma((3,)),
            dma((3,)),
            dma((2, 3)),
            dma((3,)),
            dma((3,)),
            dma,
            dma((2,)),
            dma((2,)),
            dma((2,)),
        ],
        compiler_params=pltpu.CompilerParams(
            collective_id=0, has_side_effects=True, vmem_limit_bytes=24 * 1024 * 1024
        ),
    )(*[pltpu.with_memory_space_constraint(a, pltpu.HBM) for a in (
        field, dw_kernel, dw_bias[None], zonal_kernel, zonal_bias[None], norm_gain[None], w_in,
        w_out, layer_scale[None],
    )])


def shards(
    field, dw_kernel, dw_bias, zonal_kernel, zonal_bias, norm_gain, w_in, w_out, layer_scale
):
    output = run(
        field[:, 0], dw_kernel, dw_bias, zonal_kernel, zonal_bias, norm_gain, w_in, w_out,
        layer_scale,
    )
    return output[:, None]


def solution(mesh):
    in_specs = (P(None, "face", "sub", None, None), P(), P(), P(), P(), P(), P(), P(), P())
    out_specs = P(None, "face", "sub", None, None)
    return jax.shard_map(shards, mesh=mesh, in_specs=in_specs, out_specs=out_specs, check_vma=False)
```

```python
import functools

import jax
import jax.numpy as jnp
import numpy as np
from jax import lax
from jax.experimental import pallas as pl
from jax.experimental.pallas import tpu as pltpu
from jax.sharding import PartitionSpec as P

MESH = pl.DeviceIdType.MESH
TAPS = 7
SIDE = 128
ALL = 128
LANES = 128
PITCH = 137
ROW = 8
TURN = 137
FACE_ROWS = 8 * TURN + 16
BASE_N = 288
LIN_ROWS = 1664
LIN_BLOCKS = 17


def hops(step):
    return sum(min(d, 4 - d) for d in step[:3])


STEPS = sorted(
    (
        (face, x, z, core)
        for face in range(4)
        for x in range(4)
        for z in range(4)
        for core in range(2)
        if face + x + z + core
    ),
    key=lambda step: (-hops(step) - 3 * (step[3] == 0)),
)


def peers(face, sub):
    for df, dx, dz, dc in STEPS:
        px = ((sub >> 3) + dx) & 3
        pz = ((sub >> 1) + dz) & 3
        pc = (sub + dc) & 1
        yield (face + df) & 3, (px << 3) + (pz << 1) + pc


def greet(sem, pf, ps):
    pl.semaphore_signal(sem, inc=1, device_id=(pf, ps), device_id_type=MESH)


def announce(face, sub):
    barrier = pltpu.get_barrier_semaphore()
    east = (face + 1) & 3
    west = (face + 3) & 3
    for n in range(1, 8):
        greet(barrier, face, (sub & 24) + ((sub + n) & 7))
    for n in range(1, 4):
        greet(barrier, face, (sub + 8 * n) & 31)
        greet(barrier, (face + n) & 3, sub)
    edge = sub & 7
    for cond, pf, ps in (
        (sub > 0, east, sub - 1),
        (sub > 0, west, sub - 1),
        (sub < 31, east, sub + 1),
        (sub < 31, west, sub + 1),
        ((edge == 7) & (sub < 31), face, sub + 1),
        ((edge == 0) & (sub > 0), face, sub - 1),
        (sub == 31, face, 0),
        (sub == 31, west, 0),
        (sub == 0, face, 31),
        (sub == 0, east, 31),
    ):
        pl.when(cond)(functools.partial(greet, barrier, pf, ps))
    inner_edge = ((edge == 0) | (edge == 7)) & (sub > 0) & (sub < 31)
    return 17 + inner_edge.astype(jnp.int32)


def exchange(face, sub, prepare, source, target, send_sem, recv_sem, ready=None):
    me = face * 32 + sub

    def push(pf, ps):
        copy = pltpu.make_async_remote_copy(
            source.at[pf * 32 + ps],
            target.at[me],
            send_sem,
            recv_sem,
            device_id=(pf, ps),
            device_id_type=MESH,
        )
        if ready is None:
            copy.start()
        else:
            pl.when(ready(pf * 32 + ps))(copy.start)

    waiting = None
    for pf, ps in peers(face, sub):
        prepare(pf, ps)
        if waiting is not None:
            push(*waiting)
        waiting = pf, ps
    push(*waiting)


def dispatch(face, sub, source, target, send_sem, recv_sem):
    me = face * 32 + sub

    for pf, ps in peers(face, sub):
        pltpu.make_async_remote_copy(
            source.at[pf * 32 + ps],
            target.at[me],
            send_sem,
            recv_sem,
            device_id=(pf, ps),
            device_id_type=MESH,
        ).start()


def all_blocks(face, sub, source, target, send_sem, recv_sem):
    return pltpu.make_async_remote_copy(
        source.at[pl.ds(0, ALL - 1)],
        target.at[pl.ds(0, ALL - 1)],
        send_sem,
        recv_sem,
        device_id=(face, sub),
        device_id_type=MESH,
    )


def kernel(
    field_hbm, dwk_hbm, dwb_hbm, zk_hbm, zb_hbm, gain_hbm, w_in_hbm, w_out_hbm, ls_hbm, out_ref,
    field_ref, dwk_ref, dwb_ref, zk_ref, zb_ref, gain_ref, w_in_ref, w_out_ref, ls_ref, load_sem,
    grid, row_lo, row_hi, cols, left1, right2, pieces, right0, left2, rim_hi, rim_lo, rim_rows,
    turned, send, recv, chain, ring, polar, lin, zlin, back_send, back_recv,
    send_sem, recv_sem, round_sem, row_sent, lo_sem, hi_sem, col_sent, left_sem, right_sem, piece_sent,
    piece_sem, rim_sent, rim_sem,
):
    face = lax.axis_index("face")
    sub = lax.axis_index("sub")
    me = face * 32 + sub
    east = (face + 1) & 3
    west = (face + 3) & 3
    first = sub == 0
    last = sub == 31
    loads = [
        pltpu.make_async_copy(source, target, load_sem.at[n])
        for n, (source, target) in enumerate((
            (field_hbm, field_ref), (dwk_hbm, dwk_ref), (dwb_hbm, dwb_ref), (zk_hbm, zk_ref),
            (zb_hbm, zb_ref), (gain_hbm, gain_ref), (w_in_hbm, w_in_ref), (w_out_hbm, w_out_ref),
            (ls_hbm, ls_ref)))
    ]
    loads[0].start()
    partners = announce(face, sub)
    for load in loads[1:]:
        load.start()

    def start(f, r, h=0):
        return (f * 12 + r * 2 + h) * PITCH + ROW

    def push(source, target, sent, got, pf, ps):
        return pltpu.make_async_remote_copy(
            source, target, sent, got, device_id=(pf, ps), device_id_type=MESH
        )

    rows = []
    for f in (2, 1, 0):
        rows.append((sub < 31, push(
            field_hbm.at[f, 3], row_lo.at[f], row_sent.at[0, f], lo_sem.at[f], face, sub + 1)))
        rows.append((sub > 0, push(
            field_hbm.at[f, 0], row_hi.at[f], row_sent.at[1, f], hi_sem.at[f], face, sub - 1)))
        if f:
            rows.append((last, push(
                field_hbm.at[f, 3], row_lo.at[f - 1], row_sent.at[0, f], lo_sem.at[f - 1],
                west if f == 1 else face, 0)))
        if f < 2:
            rows.append((first, push(
                field_hbm.at[f, 0], row_hi.at[f + 1], row_sent.at[1, f], hi_sem.at[f + 1],
                east if f == 0 else face, 31)))
    sides = []
    for d, cond in ((-1, sub > 0), (0, sub >= 0), (1, sub < 31)):
        sides.append((cond, push(
            cols.at[0], left1.at[1 - d], col_sent.at[0, 1 - d], left_sem.at[1 - d], east, sub + d)))
        sides.append((cond, push(
            cols.at[1], right2.at[1 - d], col_sent.at[1, 1 - d], right_sem.at[1 - d], west, sub + d)))
    outer = []
    outer.append(push(
        cols.at[2], rim_hi.at[sub], rim_sent.at[0], rim_sem.at[0], east, 31))
    outer.append(push(
        cols.at[3], rim_lo.at[sub], rim_sent.at[1], rim_sem.at[1], west, 0))

    pl.semaphore_wait(pltpu.get_barrier_semaphore(), partners)
    for n in range(1, 4):
        greet(round_sem.at[0], face, (sub + 8 * n) & 31)
    for cond, copy in rows:
        pl.when(cond)(copy.start)
    loads[0].wait()

    def widen(t, carry):
        f = t >> 2
        j = t & 3
        for h in range(2):
            grid[pl.ds(start(f, j + 1, h), SIDE), :] = field_ref[
                f, j, :, h * LANES : (h + 1) * LANES
            ].astype(jnp.float32)
        return carry

    for f, x in ((2, SIDE - 16), (1, 0)):
        for j in range(4):
            for h in range(2):
                grid[pl.ds(start(f, j + 1, h) + x, 16), :] = field_ref[
                    f, j, x : x + 16, h * LANES : (h + 1) * LANES
                ].astype(jnp.float32)

    def column(n, f, x):
        cols[n] = grid[pl.ds(start(f, 1) + x, 8, stride=PITCH), :].astype(jnp.bfloat16)

    column(0, 2, SIDE - 1)
    column(1, 1, 0)
    lax.fori_loop(0, 6, widen, 0)
    for cond, copy in sides:
        pl.when(cond)(copy.start)
    lax.fori_loop(6, 12, widen, 0)
    column(2, 0, SIDE - 1)
    column(3, 2, 0)

    def cut(base):
        def one(t, carry):
            for h in range(2):
                at = base + h * PITCH + 4 * t - 1
                pieces[t, h] = grid[pl.ds(at, 8), :].astype(jnp.bfloat16)
            return carry

        lax.fori_loop(0, 32, one, 0)

    pl.when(last)(lambda: cut(start(0, 4)))
    pl.when(first)(lambda: cut(start(2, 1)))
    for load in loads[1:]:
        load.wait()

    def weight(ref, tap, h):
        return ref[tap : tap + 1, h * LANES : (h + 1) * LANES]

    def partial_sum(total, f, j, h, x, size, rows):
        for i in rows:
            for k in range(3):
                at = start(f, j + i, h) + x + k - 1
                total = total + weight(dwk_ref, 3 * i + k, h) * grid[pl.ds(at, size), :]
        return total

    def slot(f, j, h):
        return f * FACE_ROWS + (2 * j + h) * TURN + j + 8

    def inside(f, carry):
        for j in range(4):
            rows = (1, 2) if j == 0 else (0, 1) if j == 3 else (0, 1, 2)
            for h in range(2):
                for x in (8, 64):
                    zero = jnp.broadcast_to(weight(dwb_ref, 0, h), (56, LANES))
                    turned[pl.ds(slot(f, j, h) + x, 56), :] = partial_sum(
                        zero, f, j, h, x, 56, rows)
        return carry

    inside(2, 0)
    pl.semaphore_wait(round_sem.at[0], 3)
    for n in range(1, 4):
        greet(round_sem.at[1], (face + n) & 3, sub)
    lax.fori_loop(0, 2, inside, 0)
    pl.semaphore_wait(round_sem.at[1], 3)
    for copy in outer:
        copy.start()

    def scatter(pf, target, got):
        def one(t, carry):
            push(pieces.at[t], target, piece_sent, got, pf, t).start()
            return carry

        lax.fori_loop(0, 32, one, 0)

    pl.when(last)(lambda: scatter(west, right0, piece_sem.at[0]))
    pl.when(first)(lambda: scatter(east, left2, piece_sem.at[1]))

    def took(ref, sem):
        push(ref, ref, row_sent.at[0, 0], sem, face, sub).wait_recv()

    def fill(f):
        pl.when((sub > 0) if f == 2 else (sub >= 0))(lambda: took(row_lo.at[f], lo_sem.at[f]))
        pl.when((sub < 31) if f == 0 else (sub >= 0))(lambda: took(row_hi.at[f], hi_sem.at[f]))
        for h in range(2):
            half = slice(h * LANES, (h + 1) * LANES)
            grid[pl.ds(start(f, 0, h), SIDE), :] = row_lo[f, :, half].astype(jnp.float32)
            grid[pl.ds(start(f, 5, h), SIDE), :] = row_hi[f, :, half].astype(jnp.float32)

    def side(f, x, ref, sem):
        for e, cond in ((0, sub > 0), (1, sub >= 0), (2, sub < 31)):
            pl.when(cond)(lambda e=e: took(ref.at[e], sem.at[e]))
        before = ref[0].astype(jnp.float32)
        after = ref[2].astype(jnp.float32)
        grid[pl.ds(start(f, 0) + x, 2, stride=PITCH), :] = before[6:8]
        grid[pl.ds(start(f, 1) + x, 8, stride=PITCH), :] = ref[1].astype(jnp.float32)
        grid[pl.ds(start(f, 5) + x, 2, stride=PITCH), :] = after[0:2]

    def next_to(f, x, other, at):
        for r, size in ((0, 8), (4, 4)):
            grid[pl.ds(start(f, r) + x, size, stride=PITCH), :] = grid[
                pl.ds(start(other, r) + at, size, stride=PITCH), :]

    def corners(f):
        def clear(r):
            for x in (-1, SIDE):
                grid[pl.ds(start(f, r) + x, 2, stride=PITCH), :] = jnp.zeros(
                    (2, LANES), jnp.float32)

        pl.when(first)(lambda: clear(0))
        pl.when(last)(lambda: clear(5))

    def redo(f, j, h, x, size):
        total = jnp.broadcast_to(weight(dwb_ref, 0, h), (size, LANES))
        turned[pl.ds(slot(f, j, h) + x, size), :] = partial_sum(
            total, f, j, h, x, size, (0, 1, 2))

    def wrap(f):
        for j in range(1, 4):
            for h in range(2):
                turned[pl.ds(slot(f, j, h) - j, j), :] = turned[
                    pl.ds(slot(f, j, h) + SIDE - j, j), :]

    def around(f):
        for j in range(4):
            for h in range(2):
                for x in (0, SIDE - 8):
                    redo(f, j, h, x, 8)
                if j in (0, 3):
                    for x in (8, 64):
                        at = pl.ds(slot(f, j, h) + x, 56)
                        turned[at, :] = partial_sum(
                            turned[at, :], f, j, h, x, 56, (0,) if j == 0 else (2,))
        wrap(f)

    side(2, SIDE, right2, right_sem)
    side(1, -1, left1, left_sem)
    fill(2)
    corners(2)
    around(2)
    fill(1)
    next_to(1, SIDE, 0, 0)
    corners(1)
    around(1)

    high = (0, 1, 2)
    low = (2, 0, 1)
    row_in = lax.broadcasted_iota(jnp.int32, (8, LANES), 0) // 2

    def send_family(g, ready=None):
        def pack(pf, ps):
            c = pf * 32 + ps
            t = (c - 4 * sub) & (ALL - 1)
            above = turned[pl.ds(high[g] * FACE_ROWS + 8 + t, 8, stride=TURN), :]
            below = turned[pl.ds(low[g] * FACE_ROWS + 8 + t, 8, stride=TURN), :]
            send[g, c] = jnp.where(row_in + 4 * sub > c, above, below).astype(jnp.bfloat16)

        exchange(
            face, sub, pack, send.at[g], recv.at[g], send_sem.at[g], recv_sem.at[g], ready)
        pack(face, sub)
        recv[g, me] = send[g, me]
        return pack

    send_family(2)
    fill(0)
    next_to(0, -1, 1, SIDE - 1)
    next_to(1, SIDE, 0, 0)
    corners(0)
    corners(1)
    around(0)
    for j in (0, 3):
        for h in range(2):
            redo(1, j, h, SIDE - 8, 8)
    wrap(1)
    rim_device = first | last
    pack_1 = send_family(1, lambda owner: (owner != ALL - 1) | ~rim_device)

    def rim(ref, sem, f, r):
        took(ref, sem)
        rim_rows[...] = ref[...].astype(jnp.float32).reshape(2 * SIDE, LANES)
        for h in range(2):
            grid[pl.ds(start(f, r, h), SIDE), :] = rim_rows[pl.ds(h, SIDE, stride=2), :]

    pl.when(first)(lambda: rim(rim_lo, rim_sem.at[1], 2, 0))
    pl.when(last)(lambda: rim(rim_hi, rim_sem.at[0], 0, 5))

    took(right0, piece_sem.at[0])
    took(left2, piece_sem.at[1])
    for f, x, ref in ((0, SIDE, right0), (2, -1, left2)):
        for h in range(2):
            grid[pl.ds(start(f, 0, h) + x, 6, stride=2 * PITCH), :] = ref[h].astype(jnp.float32)[:6]

    corners(0)
    corners(2)

    def redo_row(f, j):
        for h in range(2):
            for x in (0, 64):
                redo(f, j, h, x, 64)

    pl.when(last)(lambda: redo_row(0, 3))
    pl.when(first)(lambda: redo_row(2, 0))
    for j in range(4):
        for h in range(2):
            redo(0, j, h, SIDE - 8, 8)
    wrap(0)

    def pack_last():
        pack_1(3, 31)
        recv[1, me] = send[1, me]

    pl.when(rim_device)(pack_last)
    for j in range(4):
        for h in range(2):
            redo(2, j, h, 0, 8)
    pl.when(rim_device & (me != ALL - 1))(
        push(
            send.at[1, ALL - 1], recv.at[1, me], send_sem.at[1], recv_sem.at[1], 3, 31
        ).start)
    send_family(0)

    c = me
    def coeff(ref, k):
        lo = jnp.broadcast_to(ref[k : k + 1, :LANES], (8, LANES))
        hi = jnp.broadcast_to(ref[k : k + 1, LANES:], (8, LANES))
        odd = lax.rem(lax.broadcasted_iota(jnp.int32, (8, LANES), 0), 2) == 1
        return jnp.where(odd, hi, lo)

    taps = [coeff(zk_ref, k) for k in range(TAPS)]
    bias = coeff(zb_ref, 0)

    def blend(terms):
        products = [tap * term for tap, term in zip(taps, terms)]
        return ((products[0] + products[1]) + (products[2] + products[3])) + (
            (products[4] + products[5]) + (products[6] + bias))

    def arrive(g):
        all_blocks(face, sub, send.at[g], recv.at[g], send_sem.at[g], recv_sem.at[g]).wait_recv()

    def depart(g):
        back_recv[g, me] = back_send[g, me]
        dispatch(
            face, sub, back_send.at[g], back_recv.at[g], send_sem.at[3 + g], recv_sem.at[3 + g])

    block_row = 4 * lax.broadcasted_iota(jnp.int32, (8, 8, LANES), 0) + (
        lax.broadcasted_iota(jnp.int32, (8, 8, LANES), 1) // 2)

    for g in (2, 1):
        arrive(g)

        def unpack(b, carry, g=g):
            at = pl.multiple_of(8 * b, 8)
            i = (3 - (b >> 2)) * 32 + 8 * (b & 3)
            rows = recv[g, pl.ds(i, 8)].astype(jnp.float32)
            if g == 2:
                before = recv[g, pl.ds((i + 96) & (ALL - 1), 8)].astype(jnp.float32)
                rows = jnp.where(block_row + 32 * (b & 3) > c, before, rows)
            chain[pl.ds(at + 3, 8)] = rows
            return carry

        lax.fori_loop(0, 16, unpack, 0, unroll=2)
        for e in range(3):
            chain[e] = chain[ALL + e]
            chain[ALL + 3 + e] = chain[3 + e]

        def stencil_ring(b, carry, g=g):
            at = 8 * b
            i = (3 - (b >> 2)) * 32 + 8 * (b & 3)
            window = [chain[at + n] for n in range(14)]
            for n in range(8):
                total = blend(window[n : n + 7][::-1])
                if g == 1:
                    back_send[g, i + n] = total.astype(jnp.bfloat16)
                else:
                    ring[i + n] = total
            return carry

        lax.fori_loop(0, 16, stencil_ring, 0)
        if g == 2:

            def regroup(b, carry):
                rows = ring[pl.ds(8 * b, 8)]
                after = ring[pl.ds((8 * b + 32) & (ALL - 1), 8)]
                back_send[2, pl.ds(8 * b, 8)] = jnp.where(
                    block_row + 32 * (b & 3) > c, after, rows).astype(jnp.bfloat16)
                return carry

            lax.fori_loop(0, 16, regroup, 0, unroll=2)
        depart(g)

    arrive(0)

    def lay(b, carry):
        rows = recv[0, pl.ds(8 * b, 8)].astype(jnp.float32)
        polar[pl.ds(pl.multiple_of(64 * b, 64), 64), :] = rows.reshape(64, LANES)
        return carry

    lax.fori_loop(0, 16, lay, 0, unroll=2)
    arc_n = SIDE - 1 - c
    arc_s = c + 1
    base_s = BASE_N + 8 * arc_n + 48
    for q in range(4):
        lin[pl.ds(BASE_N + (3 - q) * 2 * arc_n - 2 * (c + 1), 256), :] = polar[
            q * 256 : (q + 1) * 256, :
        ]
    for q in (3, 2, 1, 0):
        lin[pl.ds(base_s + (3 - q) * 2 * arc_s, 256), :] = polar[q * 256 : (q + 1) * 256, :]
    for base, size in ((BASE_N, 8 * arc_n), (base_s, 8 * arc_s)):
        for e in range(3):
            lin[pl.ds(base + size + 8 * e, 8), :] = lin[pl.ds(base + 8 * e, 8), :]
        for e in range(1, 4):
            lin[pl.ds(base - 8 * e, 8), :] = lin[pl.ds(base - 8 * e + size, 8), :]


    def stencil_lin(v, carry):
        at = pl.multiple_of(BASE_N + 64 * v, 8)
        window = [lin[pl.ds(pl.multiple_of(at + 8 * (n - 3), 8), 8), :] for n in range(14)]
        for n in range(8):
            zlin[pl.ds(pl.multiple_of(at + 8 * n, 8), 8), :] = blend(window[n : n + 7][::-1])
        return carry

    lax.fori_loop(0, LIN_BLOCKS, stencil_lin, 0)
    row_256 = lax.broadcasted_iota(jnp.int32, (256, LANES), 0) // 2
    for q in range(4):
        from_n = zlin[pl.ds(BASE_N + (3 - q) * 2 * arc_n - 2 * (c + 1), 256), :]
        from_s = zlin[pl.ds(base_s + (3 - q) * 2 * arc_s, 256), :]
        back_send[0, pl.ds(32 * q, 32)] = (
            jnp.where(row_256 > c, from_n, from_s).reshape(32, 8, LANES).astype(jnp.bfloat16))
    depart(0)

    gain = gain_ref[...]
    scale = ls_ref[...]
    w_in = w_in_ref[...]
    w_out = w_out_ref[...]
    column = lax.broadcasted_iota(jnp.int32, (SIDE, 2 * LANES), 0)

    def mlp(g, j, carry):
        base = g * FACE_ROWS + 2 * j * TURN + j + 8
        values = jnp.concatenate(
            [turned[pl.ds(base, SIDE), :], turned[pl.ds(base + TURN, SIDE), :]], axis=1
        )
        mean = jnp.mean(values, -1, keepdims=True)
        centred = values - mean
        spread = jnp.mean(jnp.square(centred), -1, keepdims=True)
        normed = (centred * lax.rsqrt(spread + 1e-06) * gain).astype(jnp.bfloat16)
        pre = jnp.dot(normed, w_in, preferred_element_type=jnp.float32)
        hidden = (0.5 * pre * (1.0 + lax.erf(pre * np.float32(np.sqrt(0.5))))).astype(jnp.bfloat16)
        branch = jnp.dot(hidden, w_out, preferred_element_type=jnp.float32)
        upper = column + 4 * sub + j >= SIDE
        source = jnp.where(
            upper, field_ref[high[g], j].astype(jnp.float32), field_ref[low[g], j].astype(jnp.float32))
        result = source + scale * branch
        for f, kept in ((high[g], upper), (low[g], jnp.logical_not(upper))):
            seen = (g, f) in ((1, 1), (0, 0), (0, 2))
            row = jnp.where(kept, result, out_ref[f, j].astype(jnp.float32)) if seen else result
            out_ref[f, j] = row.astype(jnp.bfloat16)
        return carry

    for g in (2, 1, 0):
        all_blocks(
            face, sub, back_send.at[g], back_recv.at[g], send_sem.at[3 + g], recv_sem.at[3 + g]
        ).wait_recv()

        def unturn(i, carry, g=g):
            t = (i - 4 * sub) & (ALL - 1)
            turned[pl.ds(g * FACE_ROWS + 8 + t, 8, stride=TURN), :] = back_recv[g, i].astype(
                jnp.float32)
            return carry

        lax.fori_loop(0, ALL, unturn, 0, unroll=8)
        for j in range(1, 4):
            for h in range(2):
                turned[pl.ds(slot(g, j, h) + SIDE - j, j), :] = turned[
                    pl.ds(slot(g, j, h) - j, j), :]
        lax.fori_loop(0, 4, functools.partial(mlp, g), 0, unroll=4)

    for cond, copy in rows + sides:
        pl.when(cond)(copy.wait_send)
    for copy in outer:
        copy.wait_send()
    pl.when(first | last)(
        lambda: push(pieces, pieces, piece_sent, piece_sem.at[0], face, sub).wait_send())
    for g in range(3):
        all_blocks(face, sub, send.at[g], recv.at[g], send_sem.at[g], recv_sem.at[g]).wait_send()
        all_blocks(
            face, sub, back_send.at[g], back_recv.at[g], send_sem.at[3 + g], recv_sem.at[3 + g]
        ).wait_send()


def run(field, dw_kernel, dw_bias, zonal_kernel, zonal_bias, norm_gain, w_in, w_out, layer_scale):
    vmem = pl.BlockSpec(memory_space=pltpu.VMEM)
    lines = pltpu.VMEM((3, SIDE, 2 * LANES), jnp.bfloat16)
    tiles = lambda *lead: pltpu.VMEM((*lead, 8, LANES), jnp.bfloat16)
    rows = lambda n: pltpu.VMEM((n, LANES), jnp.float32)
    vector = pltpu.VMEM((1, 2 * LANES), jnp.float32)
    blocks = pltpu.VMEM((3, ALL, 8, LANES), jnp.bfloat16)
    dma = pltpu.SemaphoreType.DMA
    return pl.pallas_call(
        kernel,
        out_shape=jax.ShapeDtypeStruct(field.shape, jnp.bfloat16),
        in_specs=[pl.BlockSpec(memory_space=pltpu.HBM)] * 9,
        out_specs=vmem,
        scratch_shapes=[
            pltpu.VMEM(field.shape, field.dtype),
            pltpu.VMEM(dw_kernel.shape, jnp.float32),
            vector,
            pltpu.VMEM(zonal_kernel.shape, jnp.float32),
            vector,
            vector,
            pltpu.VMEM(w_in.shape, w_in.dtype),
            pltpu.VMEM(w_out.shape, w_out.dtype),
            vector,
            dma((9,)),
            rows(36 * PITCH + 16),
            lines,
            lines,
            tiles(4),
            tiles(3),
            tiles(3),
            tiles(32, 2),
            tiles(2),
            tiles(2),
            tiles(32),
            tiles(32),
            rows(2 * SIDE),
            rows(3 * FACE_ROWS + 8),
            blocks,
            blocks,
            pltpu.VMEM((ALL + 6, 8, LANES), jnp.float32),
            pltpu.VMEM((ALL, 8, LANES), jnp.float32),
            rows(1024),
            rows(LIN_ROWS),
            rows(LIN_ROWS),
            blocks,
            blocks,
            dma((6,)),
            dma((6,)),
            pltpu.SemaphoreType.REGULAR((2,)),
            dma((2, 3)),
            dma((3,)),
            dma((3,)),
            dma((2, 3)),
            dma((3,)),
            dma((3,)),
            dma,
            dma((2,)),
            dma((2,)),
            dma((2,)),
        ],
        compiler_params=pltpu.CompilerParams(
            collective_id=0, has_side_effects=True, vmem_limit_bytes=24 * 1024 * 1024
        ),
    )(*[pltpu.with_memory_space_constraint(a, pltpu.HBM) for a in (
        field, dw_kernel, dw_bias[None], zonal_kernel, zonal_bias[None], norm_gain[None], w_in,
        w_out, layer_scale[None],
    )])


def shards(
    field, dw_kernel, dw_bias, zonal_kernel, zonal_bias, norm_gain, w_in, w_out, layer_scale
):
    output = run(
        field[:, 0], dw_kernel, dw_bias, zonal_kernel, zonal_bias, norm_gain, w_in, w_out,
        layer_scale,
    )
    return output[:, None]


def solution(mesh):
    in_specs = (P(None, "face", "sub", None, None), P(), P(), P(), P(), P(), P(), P(), P())
    out_specs = P(None, "face", "sub", None, None)
    return jax.shard_map(shards, mesh=mesh, in_specs=in_specs, out_specs=out_specs, check_vma=False)
```
